32 devices in a mesh: narrow: 4 (over z), wide: 8 (over y, x, core).
Axes of the slice: x: 2, y: 2, z: 4, core: 2. Of those that a mesh axis runs over, the one named last changes fastest.
Arguments:
- tokens: bfloat16 [12288, 640], P('wide'), may hold values from -6 to 6
- cotangent: bfloat16 [12288, 640], P('wide'), may hold values from -6 to 6
- seq_lens: int32 [8, 16], P('wide'), may hold values from 1 to 1024, 1536 in all within a row
- norm_gains: bfloat16 [2, 640], replicated, may hold values from 0.099609375 to 1.8984375
- norm_shifts: bfloat16 [2, 640], replicated, may hold values from -3 to 3
- w_qkv: bfloat16 [3, 640, 640], P(None, 'wide', 'narrow'), may hold values from -0.25 to 0.25
- w_attn_out: bfloat16 [640, 640], P('narrow', 'wide'), may hold values from -2 to 2
- w_ffn_in: bfloat16 [640, 5120], P('narrow', 'wide'), may hold values from -0.25 to 0.25
- w_ffn_down: bfloat16 [640, 5120], P('narrow', 'wide'), may hold values from -0.078125 to 0.078125
Outputs:
- layer_out: bfloat16 [12288, 640], P('wide')
- input_grad: bfloat16 [12288, 640], P('wide')
- grad_norm_gains: float32 [2, 640], P(None, 'wide')
- grad_norm_shifts: float32 [2, 640], P(None, 'wide')
- grad_qkv: float32 [3, 640, 640], P(None, 'wide', 'narrow')
- grad_attn_out: float32 [640, 640], P('narrow', 'wide')
- grad_ffn_in: float32 [640, 5120], P('narrow', 'wide')
- grad_ffn_down: float32 [640, 5120], P('narrow', 'wide')
The draws below stay inside these ranges and needn't reach their ends.
Inputs may be any that keep to these rules, and one draw needn't show every extreme that they name: `seq_lens`: each row lists the lengths of the 16 sequences packed end to end in that index's 1536 slots; a row sums to 1536 and its largest entry is exactly 1024.
All inputs are finite; a program needn't handle non-finite values.
Results may differ from the reference program's by a relative error of at most 0.015.
Values may be sent and summed in bfloat16 or wider, within the bound.
No kernel may reach another device: no remote copies, remote signals or barrier semaphores. Data moves between devices by JAX's collectives and lax.ppermute only.
A program may use at most 128 MiB of HBM per device.

```python
import math
import jax
import jax.numpy as jnp
import numpy as np
from jax import lax

D = 640
HD = 32
FF = 5120
TOK_W = 1536
SEQS = 16
LONGEST = 1024
QBLK = 512
TOKENS = 12288
N_WIDE = 8


def raised(array, key, source, target, parts, factor):
    owner, partner = [(jnp.arange(array.shape[axis_at]) // (array.shape[axis_at] // parts)).reshape([-1 if axis == axis_at else 1 for axis in range(array.ndim)]) for axis_at in (source, target)]
    chosen = jax.random.permutation(key, parts)[partner]
    strong = (owner == chosen) | (owner == (partner + parts // 2) % parts)
    return jnp.where(strong, factor * array, array)


def steps_of(rng, dims, pieces, least, largest):
    def one(dim, shards_of):
        heights = jax.random.uniform(jax.random.fold_in(jax.random.fold_in(rng, 6), dim), (shards_of,), jnp.float32, least / len(pieces), largest / len(pieces))
        return jnp.repeat(jnp.exp(heights), dims[dim] // shards_of).reshape((-1,) + (1,) * (len(dims) - dim - 1))

    level = one(*pieces[0])
    for cut in pieces[1:]:
        level = level * one(*cut)
    return level


def length_profile(count, total, reach, lean):
    loads = [(1 << 20) // math.isqrt(grade ** lean) + 1 for grade in range(2, count + 1)]
    surplus, counts = total - reach - (count - 1), [1] * (count - 1)
    while surplus > 0:
        free = [i for i in range(count - 1) if counts[i] < reach]
        pool, remaining = sum([loads[i] for i in free]), surplus
        for i in free:
            extra = min(reach - counts[i], max(1, remaining * loads[i] // pool), surplus)
            counts[i] = counts[i] + extra
            surplus = surplus - extra
    return np.array([reach] + counts)


def uneven_parts(own_key, amount, total, reach, slope):
    if amount == 2:
        one = jax.random.randint(own_key, (), max(1, total - reach), min(reach, total - 1) + 1)
        return jnp.stack([one, total - one])
    tallies = jnp.asarray(length_profile(amount, total, reach, slope), jnp.int32)
    couples = (amount - 1) // 2
    giver, receiver = tallies[1:1 + 2 * couples:2], tallies[2:2 + 2 * couples:2]
    room = jnp.minimum(giver - 1, reach - receiver)
    passed = jax.random.randint(jax.random.fold_in(own_key, 1), (couples,), 0, 1 << 20) % (room + 1)
    tallies = tallies.at[1:1 + 2 * couples:2].set(giver - passed).at[2:2 + 2 * couples:2].set(receiver + passed)
    return tallies[jax.random.permutation(jax.random.fold_in(own_key, 2), amount)]


def centred(key, extent, scale, limit, cuts=(), kind=jnp.bfloat16):
    factor_of = steps_of(key, extent, cuts, -0.22, 0.18) if cuts else 1.0
    result = jax.random.normal(key, extent, jnp.float32) * scale * factor_of
    return jnp.minimum(jnp.maximum(result, -limit), limit).astype(kind)


def gaussian_with(key, extent, width, bound, shards, heavy, kind=jnp.bfloat16):
    array = width * jax.random.normal(key, extent, jnp.float32)
    if shards:
        array = array * steps_of(key, extent, shards, -0.22, 0.18)
    return jnp.clip(raised(array, jax.random.fold_in(key, 3), *heavy), -bound, bound).astype(kind)


def setup_inputs(seed: int = 0) -> dict:
    seeds = jax.random.split(jax.random.key(seed), 10)
    return {
        "tokens": gaussian_with(seeds[0], (TOKENS, D), 1.0, 6.0, ((0, 8),), (0, 1, 8, 2.0)),
        "cotangent": gaussian_with(seeds[1], (TOKENS, D), 1.0, 6.0, ((0, 8),), (0, 1, 8, 2.0)),
        "seq_lens": jax.vmap(lambda own: uneven_parts(own, SEQS, TOK_W, LONGEST, 2))(jax.random.split(seeds[2], N_WIDE)).reshape((N_WIDE, SEQS)).astype(jnp.int32),
        "norm_gains": jnp.clip(1.0 + 0.18 * jax.random.normal(seeds[3], (2, D), jnp.float32), 0.099609375, 1.8984375).astype(jnp.bfloat16),
        "norm_shifts": centred(seeds[4], (2, D), 0.5, 3.0),
        "w_qkv": centred(seeds[5], (3, D, D), D ** -0.5, 0.25, ((1, 8), (2, 4))),
        "w_attn_out": centred(seeds[6], (D, D), (D // 64) ** -0.5, 2.0, ((0, 4), (1, 8))),
        "w_ffn_in": centred(seeds[7], (D, FF), D ** -0.5, 0.25, ((0, 4), (1, 8))),
        "w_ffn_down": centred(seeds[8], (D, FF), FF ** -0.5, 0.078125, ((0, 4), (1, 8))),
    }


EPS = 1e-05
HIGH = lax.Precision.HIGHEST

@jax.custom_vjp
def low(v):
    return lax.optimization_barrier(v.astype(jnp.bfloat16)).astype(jnp.float32)

@jax.custom_vjp
def low_back(v):
    return v

def low_keep(v):
    return (low(v), None)

def low_pass(kept, grad):
    return (grad,)

def back_keep(v):
    return (v, None)

def back_low(kept, grad):
    return (low(grad),)
low.defvjp(low_keep, low_pass)
low_back.defvjp(back_keep, back_low)

def layer_norm(rows, gain, shift):
    center = rows - lax.optimization_barrier(jnp.mean(rows, axis=-1, keepdims=True))
    spread = lax.optimization_barrier(jnp.mean(center * center, axis=-1, keepdims=True))
    return center * lax.rsqrt(spread + EPS) * gain + shift

def segment_ids(lengths, count):
    ends = jnp.cumsum(lengths, dtype=jnp.int32)
    position = jnp.arange(count, dtype=jnp.int32)
    return lax.optimization_barrier(jnp.sum((position[:, None] >= ends[None, :]).astype(jnp.int32), axis=1))

def bucket_forward(params, rows, lengths):
    gains, shifts, wqkv, wout, win, wdown = params
    count = rows.shape[0]
    segment = segment_ids(lengths, count)
    normed = low(layer_norm(rows, gains[0], shifts[0]))
    proj = jnp.einsum('td,jde->jte', normed, wqkv, precision=HIGH)
    proj = low(low_back(proj))
    heads = D // HD
    scale = HD ** (-0.5)

    def split(arr):
        return arr.reshape(count, heads, HD).transpose(1, 0, 2)
    qh, kh, vh = (split(proj[0]), split(proj[1]), split(proj[2]))

    def block(start):
        qb = lax.dynamic_slice_in_dim(qh, start, QBLK, 1)
        sb = lax.dynamic_slice_in_dim(segment, start, QBLK, 0)
        scores = low_back(jnp.einsum('hqd,hkd->hqk', qb, kh, precision=HIGH) * scale)
        scores = jnp.where((sb[:, None] == segment[None, :])[None], scores, -1e+30)
        top = lax.optimization_barrier(jnp.max(scores, axis=2, keepdims=True))
        expd = jnp.exp(scores - top)
        weights = low(expd / lax.optimization_barrier(jnp.sum(expd, axis=2, keepdims=True)))
        return jnp.einsum('hqk,hkd->hqd', weights, vh, precision=HIGH)
    starts = jnp.arange(count // QBLK, dtype=jnp.int32) * QBLK
    outs = lax.map(jax.checkpoint(block), starts)
    attended = outs.transpose(0, 2, 1, 3).reshape(count, D)
    attended = low(low_back(attended))
    mixed = low_back(jnp.dot(attended, wout, precision=HIGH))
    middle = rows + mixed
    normed_two = low(layer_norm(middle, gains[1], shifts[1]))
    hidden = low_back(jnp.dot(normed_two, win, precision=HIGH))
    act = low(jax.nn.gelu(hidden, approximate=False))
    branch = lax.dot_general(act, wdown, (((1,), (1,)), ((), ())), precision=HIGH)
    return middle + branch

def reference(tokens, cotangent, seq_lens, norm_gains, norm_shifts, w_qkv, w_attn_out, w_ffn_in, w_ffn_down):
    params = tuple((arr.astype(jnp.float32) for arr in (norm_gains, norm_shifts, w_qkv, w_attn_out, w_ffn_in, w_ffn_down)))

    def layer(inputs, weights):
        buckets = inputs.reshape(N_WIDE, TOK_W, D)

        def step(carry, item):
            return (carry, bucket_forward(weights, item[0], item[1]))
        _, outs = lax.scan(jax.checkpoint(step), jnp.zeros((), jnp.float32), (buckets, seq_lens))
        return outs.reshape(TOKENS, D)
    out, pull = jax.vjp(layer, tokens.astype(jnp.float32), params)
    dinput, dparams = pull(cotangent.astype(jnp.float32))
    return (out.astype(jnp.bfloat16), dinput.astype(jnp.bfloat16), dparams[0], dparams[1], dparams[2], dparams[3], dparams[4], dparams[5])
```

```python
from functools import partial

import jax
import jax.numpy as jnp
from jax import lax
from jax.experimental import pallas as pl
from jax.experimental.pallas import tpu as pltpu
from jax.sharding import PartitionSpec as P

HD = 32
EPS = 1e-05
LOG2E = 1.4426950408889634
SCALE = HD ** (-0.5)
BQ = 256
BK = 256
BF16 = jnp.bfloat16
F32 = jnp.float32
VMEM_LIMIT = 56 * 1024 * 1024


def vmem(*shape):
    return pl.BlockSpec(shape, None) if shape else pl.BlockSpec(memory_space=pltpu.VMEM)


def dot(a, b):
    return jnp.dot(a, b, preferred_element_type=F32)


def dot_nt(a, b):
    return lax.dot_general(a, b, (((1,), (1,)), ((), ())), preferred_element_type=F32)


def normalized(rows):
    center = rows - jnp.mean(rows, axis=-1, keepdims=True)
    spread = jnp.mean(center * center, axis=-1, keepdims=True)
    inverse = lax.rsqrt(spread + EPS)
    return center * inverse, inverse


def norm_backward(rows, gain, grad):
    unit, inverse = normalized(rows)
    scaled = grad * gain
    inner = scaled - jnp.mean(scaled, axis=-1, keepdims=True)
    inner = inner - unit * jnp.mean(scaled * unit, axis=-1, keepdims=True)
    return inverse * inner, grad * unit


def project_kernel(
    lens, x_ref, gain_ref, shift_ref, w_ref,
    xn_ref, q_ref, k_ref, qt_ref, kt_ref, vt_ref, segc_ref, segr_ref, bounds_ref,
):
    block = pl.program_id(0)
    first = block * BQ
    last = first + BQ - 1
    heads = q_ref.shape[0]
    end = jnp.int32(0)
    low = jnp.int32(0)
    high = jnp.int32(pl.num_programs(0) * BQ)
    rows = first + lax.broadcasted_iota(jnp.int32, segc_ref.shape, 0)
    cols = first + lax.broadcasted_iota(jnp.int32, segr_ref.shape, 1)
    seg_rows = jnp.zeros(segc_ref.shape, jnp.int32)
    seg_cols = jnp.zeros(segr_ref.shape, jnp.int32)
    for item in range(lens.shape[1]):
        end = end + lens[0, item]
        low = jnp.where(end <= first, end, low)
        high = jnp.where((end > last) & (end < high), end, high)
        seg_rows = seg_rows + (rows >= end).astype(jnp.int32)
        seg_cols = seg_cols + (cols >= end).astype(jnp.int32)
    segc_ref[...] = seg_rows
    segr_ref[...] = seg_cols
    bounds_ref[block, 0] = lax.div(low, jnp.int32(BK))
    bounds_ref[block, 1] = lax.div(high + (BK - 1), jnp.int32(BK))
    unit, _ = normalized(x_ref[...].astype(F32))
    xn = (unit * gain_ref[0:1, :].astype(F32) + shift_ref[0:1, :].astype(F32)).astype(BF16)
    xn_ref[...] = xn
    for item, (rows_ref, cols_ref) in enumerate(((q_ref, qt_ref), (k_ref, kt_ref), (None, vt_ref))):
        full = dot(xn, w_ref[item])
        cols_ref[...] = full.T.astype(BF16)
        if rows_ref is not None:
            low_rows = full.astype(BF16)
            for head in range(heads):
                rows_ref[head] = low_rows[:, head * HD : (head + 1) * HD]


def project(lens, tokens, gains, shifts, weights):
    count, dim = tokens.shape
    width = weights.shape[2]
    heads = width // HD
    blocks = count // BQ
    per_head = pl.BlockSpec((heads, BQ, HD), lambda i: (0, i, 0))
    turned = pl.BlockSpec((width, BQ), lambda i: (0, i))
    fixed2 = pl.BlockSpec((2, dim), lambda i: (0, 0))
    return pl.pallas_call(
        project_kernel,
        grid=(blocks,),
        in_specs=[
            pl.BlockSpec(memory_space=pltpu.SMEM),
            pl.BlockSpec((BQ, dim), lambda i: (i, 0)),
            fixed2,
            fixed2,
            pl.BlockSpec((3, dim, width), lambda i: (0, 0, 0)),
        ],
        out_specs=[
            pl.BlockSpec((BQ, dim), lambda i: (i, 0)),
            per_head,
            per_head,
            turned,
            turned,
            turned,
            pl.BlockSpec((BQ, 128), lambda i: (i, 0)),
            pl.BlockSpec((8, BQ), lambda i: (0, i)),
            pl.BlockSpec(memory_space=pltpu.SMEM),
        ],
        out_shape=[
            jax.ShapeDtypeStruct((count, dim), BF16),
            jax.ShapeDtypeStruct((heads, count, HD), BF16),
            jax.ShapeDtypeStruct((heads, count, HD), BF16),
            jax.ShapeDtypeStruct((width, count), BF16),
            jax.ShapeDtypeStruct((width, count), BF16),
            jax.ShapeDtypeStruct((width, count), BF16),
            jax.ShapeDtypeStruct((count, 128), jnp.int32),
            jax.ShapeDtypeStruct((8, count), jnp.int32),
            jax.ShapeDtypeStruct((blocks, 2), jnp.int32),
        ],
        compiler_params=pltpu.CompilerParams(vmem_limit_bytes=VMEM_LIMIT),
        cost_estimate=pl.CostEstimate(
            flops=2 * count * dim * 3 * width, bytes_accessed=4 * count * dim, transcendentals=0
        ),
        name="project",
    )(lens, tokens, gains, shifts, weights)


def spread_lanes(column, width):
    return jnp.concatenate([column] * (width // 128), axis=1) if width > 128 else column


def attend_kernel(
    first, heads, bounds, segc_ref, segr_ref, k_ref, qt_ref, vt_ref, part_ref, ot_ref, lse_ref
):
    count = segc_ref.shape[0]
    factor = SCALE * LOG2E

    def q_block(block, _):
        start = pl.multiple_of(block * BQ, BQ)
        seg_q = segr_ref[0:1, pl.ds(start, BQ)]
        queries = [
            qt_ref[(first + h) * HD : (first + h + 1) * HD, pl.ds(start, BQ)] for h in range(heads)
        ]

        def k_block(item, carry):
            at = pl.multiple_of(item * BK, BK)
            allowed = spread_lanes(segc_ref[pl.ds(at, BK), :], BQ) == seg_q
            out = []
            scores = [dot(k_ref[first + h, pl.ds(at, BK), :], queries[h]) for h in range(heads)]
            scores = [jnp.where(allowed, value, -1e30) for value in scores]
            fresh = [
                jnp.maximum(carry[h][0], jnp.max(scores[h], axis=0, keepdims=True))
                for h in range(heads)
            ]
            expd = [jnp.exp2((scores[h] - fresh[h]) * factor) for h in range(heads)]
            for h in range(heads):
                top, total, acc = carry[h]
                fade = jnp.exp2((top - fresh[h]) * factor)
                total = total * fade + jnp.sum(expd[h], axis=0, keepdims=True)
                rows = vt_ref[(first + h) * HD : (first + h + 1) * HD, pl.ds(at, BK)]
                acc = acc * fade + dot(rows, expd[h].astype(BF16))
                out.append((fresh[h], total, acc))
            return tuple(out)

        empty = (
            jnp.full((1, BQ), -1e30, F32),
            jnp.zeros((1, BQ), F32),
            jnp.zeros((HD, BQ), F32),
        )
        done = lax.fori_loop(bounds[block, 0], bounds[block, 1], k_block, (empty,) * heads)
        for h in range(heads):
            top, total, acc = done[h]
            ot_ref[h * HD : (h + 1) * HD, pl.ds(start, BQ)] = acc / total
            lse_ref[h : h + 1, pl.ds(start, BQ)] = top * factor + jnp.log(total) * LOG2E
        return 0

    lax.fori_loop(0, count // BQ, q_block, 0)
    parts = part_ref.shape[0]
    size = count // parts
    for part in range(parts):
        part_ref[part] = ot_ref[:, part * size : (part + 1) * size].astype(BF16)


def attend(first, heads, parts, tables, k_rows, q_cols, v_cols):
    segc, segr, bounds = tables
    count = segc.shape[0]
    return pl.pallas_call(
        partial(attend_kernel, first, heads),
        in_specs=[pl.BlockSpec(memory_space=pltpu.SMEM)] + [vmem()] * 5,
        out_specs=[vmem()] * 3,
        out_shape=[
            jax.ShapeDtypeStruct((parts, heads * HD, count // parts), BF16),
            jax.ShapeDtypeStruct((heads * HD, count), F32),
            jax.ShapeDtypeStruct((8, count), F32),
        ],
        compiler_params=pltpu.CompilerParams(vmem_limit_bytes=VMEM_LIMIT),
        cost_estimate=pl.CostEstimate(
            flops=heads * count * count * 300, bytes_accessed=4 * count * 640, transcendentals=0
        ),
        name=f"attend_{first}",
    )(bounds, segc, segr, k_rows, q_cols, v_cols)


def attend_back_kernel(
    first, heads, bounds, segc_ref, segr_ref, q_ref, k_ref, qt_ref, kt_ref, vt_ref,
    part_ref, ot_ref, lse_ref, out_ref, flat_ref,
    dot_ref, do_ref, stat_ref, dq_ref, dqt_ref, dkt_ref, dvt_ref,
):
    count = segc_ref.shape[0]
    factor = SCALE * LOG2E
    parts = part_ref.shape[0]
    size = count // parts
    for part in range(parts):
        dot_ref[:, part * size : (part + 1) * size] = part_ref[part]
        for h in range(heads):
            do_ref[h, part * size : (part + 1) * size, :] = part_ref[
                part, h * HD : (h + 1) * HD, :
            ].T
    dkt_ref[...] = jnp.zeros_like(dkt_ref)
    dvt_ref[...] = jnp.zeros_like(dvt_ref)

    def q_block(block, _):
        start = pl.multiple_of(block * BQ, BQ)
        spot = pl.ds(start, BQ)
        stats = [lse_ref[0:heads, spot]]
        for h in range(heads):
            lane = slice(h * HD, (h + 1) * HD)
            stats.append(
                jnp.sum(dot_ref[lane, spot].astype(F32) * ot_ref[lane, spot], axis=0, keepdims=True)
            )
        stats.append(jnp.zeros((8 - 2 * heads, BQ), F32)) if heads < 4 else None
        turned = jnp.concatenate(stats, axis=0).T
        for h in range(2 * heads):
            stat_ref[h] = jnp.broadcast_to(turned[:, h : h + 1], (BQ, 128))
        dq_ref[...] = jnp.zeros_like(dq_ref)
        seg_q = spread_lanes(segc_ref[spot, :], BK)

        def k_block(item, _):
            at = pl.multiple_of(item * BK, BK)
            here = pl.ds(at, BK)
            allowed = seg_q == segr_ref[0:1, here]
            lanes = [slice(h * HD, (h + 1) * HD) for h in range(heads)]
            owns = [slice((first + h) * HD, (first + h + 1) * HD) for h in range(heads)]
            scores = [dot(q_ref[first + h, spot, :], kt_ref[owns[h], here]) for h in range(heads)]
            dprob = [dot(do_ref[h, spot, :], vt_ref[owns[h], here]) for h in range(heads)]
            prob = [
                jnp.where(
                    allowed, jnp.exp2(scores[h] * factor - spread_lanes(stat_ref[h], BK)), 0.0
                )
                for h in range(heads)
            ]
            dscore = [
                (prob[h] * (dprob[h] - spread_lanes(stat_ref[heads + h], BK))).astype(BF16)
                for h in range(heads)
            ]
            for h in range(heads):
                dvt_ref[lanes[h], here] += dot(dot_ref[lanes[h], spot], prob[h].astype(BF16))
                dkt_ref[lanes[h], here] += dot(qt_ref[owns[h], spot], dscore[h])
                dq_ref[h] += dot(dscore[h], k_ref[first + h, here, :])
            return 0

        lax.fori_loop(bounds[block, 0], bounds[block, 1], k_block, 0)
        for h in range(heads):
            dqt_ref[h * HD : (h + 1) * HD, spot] = dq_ref[h].T * SCALE
        return 0

    lax.fori_loop(0, count // BQ, q_block, 0)
    width = heads * HD
    for item, (source, scale) in enumerate(((dqt_ref, 1.0), (dkt_ref, SCALE), (dvt_ref, 1.0))):
        value = source[...] if scale == 1.0 else source[...] * scale
        value = value.astype(BF16)
        flat_ref[item * width : (item + 1) * width, :] = value
        for part in range(parts):
            out_ref[part, item * width : (item + 1) * width, :] = value[
                :, part * size : (part + 1) * size
            ]


def attend_back(first, heads, tables, q_rows, k_rows, q_cols, k_cols, v_cols, dout, out, lse):
    segc, segr, bounds = tables
    count = segc.shape[0]
    parts = dout.shape[0]
    width = heads * HD
    return pl.pallas_call(
        partial(attend_back_kernel, first, heads),
        in_specs=[pl.BlockSpec(memory_space=pltpu.SMEM)] + [vmem()] * 10,
        out_specs=[vmem()] * 2,
        out_shape=[
            jax.ShapeDtypeStruct((parts, 3 * width, count // parts), BF16),
            jax.ShapeDtypeStruct((3 * width, count), BF16),
        ],
        scratch_shapes=[
            pltpu.VMEM((width, count), BF16),
            pltpu.VMEM((heads, count, HD), BF16),
            pltpu.VMEM((2 * heads, BQ, 128), F32),
            pltpu.VMEM((heads, BQ, HD), F32),
            pltpu.VMEM((width, count), F32),
            pltpu.VMEM((width, count), F32),
            pltpu.VMEM((width, count), F32),
        ],
        compiler_params=pltpu.CompilerParams(vmem_limit_bytes=VMEM_LIMIT),
        cost_estimate=pl.CostEstimate(
            flops=heads * count * count * 900, bytes_accessed=4 * count * 640, transcendentals=0
        ),
        name=f"attend_back_{first}",
    )(bounds, segc, segr, q_rows, k_rows, q_cols, k_cols, v_cols, dout, out, lse)


def mix_kernel(ot_ref, w_ref, x_ref, gain_ref, shift_ref, x2_ref, xn_ref, full_ref):
    tall, across, height, narrow = w_ref.shape
    for i in range(tall):
        for j in range(across):
            full_ref[i * height : (i + 1) * height, j * narrow : (j + 1) * narrow] = w_ref[i, j]
    mixed = lax.dot_general(
        ot_ref[...], full_ref[...], (((0,), (0,)), ((), ())), preferred_element_type=F32
    )
    middle = x_ref[...].astype(F32) + mixed
    x2_ref[...] = middle
    unit, _ = normalized(middle)
    xn_ref[...] = (unit * gain_ref[1:2, :].astype(F32) + shift_ref[1:2, :].astype(F32)).astype(BF16)


def mix(ot, w_pieces, rows, gains, shifts):
    count, dim = rows.shape
    return pl.pallas_call(
        mix_kernel,
        in_specs=[vmem()] * 5,
        out_specs=[vmem()] * 3,
        out_shape=[
            jax.ShapeDtypeStruct((count, dim), F32),
            jax.ShapeDtypeStruct((count, dim), BF16),
            jax.ShapeDtypeStruct((dim, dim), BF16),
        ],
        compiler_params=pltpu.CompilerParams(vmem_limit_bytes=VMEM_LIMIT),
        cost_estimate=pl.CostEstimate(
            flops=2 * count * dim * dim, bytes_accessed=8 * count * dim, transcendentals=0
        ),
        name="mix",
    )(ot, w_pieces, rows, gains, shifts)


ROWS = 256


def ffn_kernel(blocks, start, stop, *refs):
    refs = list(refs)
    xn_parts = [refs.pop(0), refs.pop(0)]
    dy_parts = [refs.pop(0), refs.pop(0)]
    weights = [(refs.pop(0), refs.pop(0)) for _ in range(blocks)]
    old = None if start else (refs.pop(0), refs.pop(0))
    y_out, dx_out = refs.pop(0), refs.pop(0)
    far_out = refs.pop(0) if stop else None
    grads = [(refs.pop(0), refs.pop(0)) for _ in range(blocks)]
    if stop:
        y_ref, dx_ref = refs.pop(0), refs.pop(0)
    else:
        y_ref, dx_ref = y_out, dx_out
    xn_ref, dy_ref, g_ref, du_ref = refs
    mine = xn_parts[0].shape[0]
    count = xn_ref.shape[0]
    for item in range(2):
        xn_ref[item * mine : (item + 1) * mine, :] = xn_parts[item][...]
        dy_ref[item * mine : (item + 1) * mine, :] = dy_parts[item][...]
    for index, ((in_ref, down_ref), (gin_ref, gdown_ref)) in enumerate(zip(weights, grads)):
        for first in range(0, count, ROWS):
            rows = slice(first, first + ROWS)
            u = dot(xn_ref[rows, :], in_ref[...])
            dg = dot(dy_ref[rows, :], down_ref[...])
            half = 0.5 + 0.5 * lax.erf(u * 0.7071067811865476)
            slope = half + u * (jnp.exp2(u * u * (-0.5 * LOG2E)) * 0.3989422804014327)
            g = (u * half).astype(BF16)
            du = (dg * slope).astype(BF16)
            g_ref[rows, :] = g
            du_ref[rows, :] = du
            y = dot_nt(g, down_ref[...])
            dx = dot_nt(du, in_ref[...])
            if index > 0:
                y = y + y_ref[rows, :]
                dx = dx + dx_ref[rows, :]
            elif old is not None:
                y = y + old[0][rows, :]
                dx = dx + old[1][rows, :]
            y_ref[rows, :] = y
            dx_ref[rows, :] = dx
        gin_ref[...] = lax.dot_general(
            xn_ref[...], du_ref[...], (((0,), (0,)), ((), ())), preferred_element_type=F32
        ).astype(BF16)
        gdown_ref[...] = lax.dot_general(
            dy_ref[...], g_ref[...], (((0,), (0,)), ((), ())), preferred_element_type=F32
        ).astype(BF16)
    if stop:
        y_out[...] = y_ref[:mine, :]
        dx_out[...] = dx_ref[:mine, :]
        far_out[0] = y_ref[mine:, :].astype(BF16)
        far_out[1] = dx_ref[mine:, :].astype(BF16)


def ffn(xn, dy, weights, sums=None, stop=False):
    mine, dim = xn[0].shape
    count = 2 * mine
    blocks = len(weights)
    hidden = weights[0][0].shape[1]
    start = sums is None
    total = jax.ShapeDtypeStruct((mine if stop else count, dim), F32)
    grad = jax.ShapeDtypeStruct((dim, hidden), BF16)
    far = [jax.ShapeDtypeStruct((2, mine, dim), BF16)] if stop else []
    args = [*xn, *dy, *(part for pair in weights for part in pair)]
    args += [] if start else list(sums)
    out_shape = [total, total] + far + [grad] * (2 * blocks)
    scratch = [pltpu.VMEM((count, dim), F32)] * 2 if stop else []
    out = pl.pallas_call(
        partial(ffn_kernel, blocks, start, stop),
        in_specs=[vmem()] * len(args),
        out_specs=[vmem()] * len(out_shape),
        out_shape=out_shape,
        scratch_shapes=scratch
        + [pltpu.VMEM((count, dim), BF16)] * 2
        + [pltpu.VMEM((count, hidden), BF16)] * 2,
        compiler_params=pltpu.CompilerParams(vmem_limit_bytes=VMEM_LIMIT),
        cost_estimate=pl.CostEstimate(
            flops=12 * count * dim * hidden * blocks,
            bytes_accessed=8 * count * dim + 8 * blocks * dim * hidden,
            transcendentals=2 * count * hidden * blocks,
        ),
        name="ffn",
    )(*args)
    head = 3 if stop else 2
    return out[:head], [tuple(out[head + 2 * i : head + 2 * i + 2]) for i in range(blocks)]


def turn_kernel(
    x2_ref, y_ref, dx_ref, far_ref, dy_ref, w_ref, ot_ref, gain_ref,
    out_ref, dx2_ref, dot_ref, gout_ref, sums_ref,
):
    middle = x2_ref[...]
    out_ref[...] = (middle + y_ref[...] + far_ref[0].astype(F32)).astype(BF16)
    grad = dx_ref[...] + far_ref[1].astype(F32)
    back, prod = norm_backward(middle, gain_ref[1:2, :].astype(F32), grad)
    dx2 = dy_ref[...].astype(F32) + back
    dx2_ref[...] = dx2
    sums_ref[...] = jnp.concatenate(
        [
            jnp.sum(prod, axis=0, keepdims=True),
            jnp.sum(grad, axis=0, keepdims=True),
            jnp.zeros((6, grad.shape[1]), F32),
        ],
        axis=0,
    )
    low = dx2.astype(BF16)
    dot_ref[...] = dot_nt(w_ref[...], low).astype(BF16)
    gout_ref[...] = lax.dot_general(
        low, ot_ref[...], (((0,), (1,)), ((), ())), preferred_element_type=F32
    ).astype(BF16)


def turn(x2, y, dx, far, dy, w_out, ot, gains):
    count, dim = x2.shape
    return pl.pallas_call(
        turn_kernel,
        in_specs=[vmem()] * 8,
        out_specs=[vmem()] * 5,
        out_shape=[
            jax.ShapeDtypeStruct((count, dim), BF16),
            jax.ShapeDtypeStruct((count, dim), F32),
            jax.ShapeDtypeStruct((dim, count), BF16),
            jax.ShapeDtypeStruct((dim, dim), BF16),
            jax.ShapeDtypeStruct((8, dim), F32),
        ],
        compiler_params=pltpu.CompilerParams(vmem_limit_bytes=VMEM_LIMIT),
        cost_estimate=pl.CostEstimate(
            flops=4 * count * dim * dim, bytes_accessed=24 * count * dim, transcendentals=0
        ),
        name="turn",
    )(x2, y, dx, far, dy, w_out, ot, gains)


def finish_kernel(parts_ref, w_ref, x_ref, dx2_ref, gain_ref, out_ref, sums_ref):
    groups, _, _, width = w_ref.shape
    total = None
    for group in range(groups):
        for item in range(3):
            term = dot(w_ref[group, item], parts_ref[group, item * width : (item + 1) * width, :])
            total = term if total is None else total + term
    grad = total.T
    back, prod = norm_backward(x_ref[...].astype(F32), gain_ref[0:1, :].astype(F32), grad)
    out_ref[...] = (dx2_ref[...] + back).astype(BF16)
    sums_ref[...] = jnp.concatenate(
        [
            jnp.sum(prod, axis=0, keepdims=True),
            jnp.sum(grad, axis=0, keepdims=True),
            jnp.zeros((6, grad.shape[1]), F32),
        ],
        axis=0,
    )


def finish(parts, w_qkv, rows, dx2, gains):
    count, dim = rows.shape
    return pl.pallas_call(
        finish_kernel,
        in_specs=[vmem()] * 5,
        out_specs=[vmem()] * 2,
        out_shape=[
            jax.ShapeDtypeStruct((count, dim), BF16),
            jax.ShapeDtypeStruct((8, dim), F32),
        ],
        compiler_params=pltpu.CompilerParams(vmem_limit_bytes=VMEM_LIMIT),
        cost_estimate=pl.CostEstimate(
            flops=6 * count * dim * dim, bytes_accessed=16 * count * dim, transcendentals=0
        ),
        name="finish",
    )(parts, w_qkv, rows, dx2, gains)


def swap(value, bit, size):
    return lax.ppermute(value, "wide", [(i, i ^ bit) for i in range(size)])


def exchange(value, axis):
    return lax.all_to_all(value, axis, 0, 0, tiled=True)


def local(
    tokens, cotangent, seq_lens, norm_gains, norm_shifts, w_qkv, w_attn_out, w_ffn_in, w_ffn_down
):
    depth = lax.axis_size("narrow")
    across = lax.axis_size("wide")
    count, dim = tokens.shape
    mine = count // depth
    width = w_qkv.shape[2]
    cols = w_ffn_in.shape[1]
    layer = lax.axis_index("narrow")
    place = lax.axis_index("wide")
    close = across == 8

    qkv = lax.all_gather(w_qkv, "wide", axis=1, tiled=True)
    pieces = lax.all_to_all(
        jnp.broadcast_to(w_attn_out[None], (depth * across,) + w_attn_out.shape),
        ("narrow", "wide"), 0, 0, tiled=True,
    ).reshape((depth, across) + w_attn_out.shape)
    stacked = lax.all_gather(
        jnp.concatenate([w_ffn_in, w_ffn_down], axis=1), "narrow", axis=0, tiled=True
    )
    if close:
        block = (stacked[:, :cols], stacked[:, cols:])
        block_x = tuple(swap(part, 2, across) for part in block)
        block_y = tuple(swap(part, 4, across) for part in block)
        block_d = (swap(block_x[0], 4, across), swap(block_y[1], 2, across))
        weights = [block, block_x, block_y, block_d]
    else:
        every = lax.all_gather(stacked, "wide", axis=0)
        every = every.reshape(across // 2, 2, dim, 2 * cols)
        every = lax.dynamic_index_in_dim(every, place % 2, 1, keepdims=False)
        flat = [
            every[:, :, at : at + cols].transpose(1, 0, 2).reshape(dim, -1) for at in (0, cols)
        ]
        weights = [
            tuple(part[:, at : at + dim] for part in flat) for at in range(0, flat[0].shape[1], dim)
        ]

    rows = lax.dynamic_slice_in_dim(tokens, layer * mine, mine, 0)
    dy = lax.dynamic_slice_in_dim(cotangent, layer * mine, mine, 0)
    dy_pair = (dy, swap(dy, 1, across))

    xn, q_rows, k_rows, q_cols, k_cols, v_cols, *tables = project(
        seq_lens, tokens, norm_gains, norm_shifts, qkv
    )
    heads = width // HD
    part, out, lse = attend(0, heads, depth, tables, k_rows, q_cols, v_cols)
    ot = exchange(part, "narrow").reshape(dim, mine)
    x2, xn2, w_out = mix(ot, pieces, rows, norm_gains, norm_shifts)
    xn_pair = (xn2, swap(xn2, 1, across))

    sums, grads_a = ffn(xn_pair, dy_pair, weights[:1])
    sums, grads_b = ffn(xn_pair, dy_pair, weights[1:-1], sums)
    (y, dx, far), grads_c = ffn(xn_pair, dy_pair, weights[-1:], sums, stop=True)
    far = swap(far, 1, across)
    out_mine, dx2, dot_cols, grad_out, norm_two = turn(
        x2, y, dx, far, dy, w_out, ot, norm_gains
    )
    layer_out = lax.all_gather(out_mine, "narrow", axis=0, tiled=True)

    dout = exchange(dot_cols.reshape(depth, width, mine), "narrow")
    back, flat_back = attend_back(
        0, heads, tables, q_rows, k_rows, q_cols, k_cols, v_cols, dout, out, lse
    )
    qkv_all = lax.all_gather(qkv, "narrow", axis=0)
    back = exchange(back, "narrow")
    in_mine, norm_one = finish(back, qkv_all, rows, dx2, norm_gains)
    input_grad = lax.all_gather(in_mine, "narrow", axis=0, tiled=True)

    grads = grads_a + grads_b + grads_c
    if close:
        own, gx, gy, gd = grads
        add = lambda *parts: sum(part.astype(F32) for part in parts).astype(BF16)
        relay_in = swap(gd[0], 2, across)
        relay_down = swap(gd[1], 4, across)
        gy_in = add(gy[0], relay_in)
        gx_down = add(gx[1], relay_down)
        from_x = (swap(gx[0], 2, across), swap(gx_down, 2, across))
        from_y = (swap(gy_in, 4, across), swap(gy[1], 4, across))
        total = jnp.concatenate([add(own[i], from_x[i], from_y[i]) for i in range(2)], axis=1)
    else:
        both = [
            jnp.concatenate([pair[i] for pair in grads], axis=1)
            .reshape(dim, across // 2, cols)
            .transpose(1, 0, 2)
            for i in range(2)
        ]
        both = jnp.concatenate(both, axis=2)[:, None]
        core = jnp.arange(2).reshape(1, 2, 1, 1) == place % 2
        both = jnp.where(core, both, jnp.zeros((), BF16)).reshape(across, dim, 2 * cols)
        total = lax.psum_scatter(both, "wide", scatter_dimension=0, tiled=False)
    total = lax.psum_scatter(total, "narrow", scatter_dimension=0, tiled=True).astype(F32)

    gqkv = lax.dot_general(
        xn, flat_back, (((0,), (1,)), ((), ())), preferred_element_type=F32
    ).astype(BF16)
    gqkv = exchange(gqkv.reshape(across, dim // across, 3 * width), "wide")
    gqkv = jnp.sum(gqkv.astype(F32), axis=0)
    gqkv = gqkv.reshape(dim // across, 3, width).transpose(1, 0, 2)

    gout = exchange(grad_out.reshape(across, dim // across, dim), "wide")
    gout = jnp.sum(gout.astype(F32), axis=0).astype(BF16)
    gout = exchange(gout.reshape(dim // across, depth, width).transpose(1, 0, 2), "narrow")
    gout = jnp.sum(gout.astype(F32), axis=0).T

    norms = jnp.concatenate([norm_one[:2], norm_two[:2]], axis=0)
    norms = lax.psum(norms, ("narrow", "wide"))
    norms = lax.dynamic_slice_in_dim(norms, place * (dim // across), dim // across, 1)
    return (
        layer_out,
        input_grad,
        norms[0::2],
        norms[1::2],
        gqkv,
        gout,
        total[:, :cols],
        total[:, cols:],
    )


def solution(mesh):
    placed = (
        P("wide", None),
        P("wide", None),
        P("wide", None),
        P(),
        P(),
        P(None, "wide", "narrow"),
        P("narrow", "wide"),
        P("narrow", "wide"),
        P("narrow", "wide"),
    )
    return jax.shard_map(
        local,
        mesh=mesh,
        in_specs=placed,
        out_specs=(
            P("wide", None),
            P("wide", None),
            P(None, "wide"),
            P(None, "wide"),
            P(None, "wide", "narrow"),
            P("narrow", "wide"),
            P("narrow", "wide"),
            P("narrow", "wide"),
        ),
        check_vma=False,
    )
```

```python
from functools import partial

import jax
import jax.numpy as jnp
from jax import lax
from jax.experimental import pallas as pl
from jax.experimental.pallas import tpu as pltpu
from jax.sharding import PartitionSpec as P

HD = 32
EPS = 1e-05
LOG2E = 1.4426950408889634
SCALE = HD ** (-0.5)
BQ = 256
BK = 256
STEP = 256
BF16 = jnp.bfloat16
F32 = jnp.float32
VMEM_LIMIT = 56 * 1024 * 1024
COST = pl.CostEstimate(flops=1000000, bytes_accessed=100000, transcendentals=0)


def vmem(*shape):
    return pl.BlockSpec(shape, None) if shape else pl.BlockSpec(memory_space=pltpu.VMEM)


def dot(a, b):
    return jnp.dot(a, b, preferred_element_type=F32)


def dot_nt(a, b):
    return lax.dot_general(a, b, (((1,), (1,)), ((), ())), preferred_element_type=F32)


def normalized(rows):
    center = rows - jnp.mean(rows, axis=-1, keepdims=True)
    spread = jnp.mean(center * center, axis=-1, keepdims=True)
    inverse = lax.rsqrt(spread + EPS)
    return center * inverse, inverse


def norm_backward(rows, gain, grad):
    unit, inverse = normalized(rows)
    scaled = grad * gain
    inner = scaled - jnp.mean(scaled, axis=-1, keepdims=True)
    inner = inner - unit * jnp.mean(scaled * unit, axis=-1, keepdims=True)
    return inverse * inner, grad * unit


def project_kernel(
    lens, x_ref, gain_ref, shift_ref, w_ref,
    unit_ref, q_ref, k_ref, qt_ref, kt_ref, vt_ref, segc_ref, segr_ref, bounds_ref, full_ref, out_ref,
):
    across, kinds, _, narrow = w_ref.shape

    @pl.when(pl.program_id(0) == 0)
    def _():
        for part in range(across):
            spot = slice(part * narrow, (part + 1) * narrow)
            for item in range(kinds - 1):
                full_ref[item, :, spot] = w_ref[part, item]
            for copy in range(out_ref.shape[0]):
                out_ref[copy, :, spot] = w_ref[part, kinds - 1]

    block = pl.program_id(0)
    first = block * BQ
    last = first + BQ - 1
    heads = q_ref.shape[0]
    end = jnp.int32(0)
    low = jnp.int32(0)
    high = jnp.int32(pl.num_programs(0) * BQ)
    rows = first + lax.broadcasted_iota(jnp.int32, segc_ref.shape, 0)
    cols = first + lax.broadcasted_iota(jnp.int32, segr_ref.shape, 1)
    seg_rows = jnp.zeros(segc_ref.shape, jnp.int32)
    seg_cols = jnp.zeros(segr_ref.shape, jnp.int32)
    for item in range(lens.shape[1]):
        end = end + lens[0, item]
        low = jnp.where(end <= first, end, low)
        high = jnp.where((end > last) & (end < high), end, high)
        seg_rows = seg_rows + (rows >= end).astype(jnp.int32)
        seg_cols = seg_cols + (cols >= end).astype(jnp.int32)
    segc_ref[...] = seg_rows
    segr_ref[...] = seg_cols
    low = lax.div(low, jnp.int32(STEP))
    high = lax.div(high + (STEP - 1), jnp.int32(STEP))
    steps = lax.div((high - low) * STEP + (BK - 1), jnp.int32(BK))
    room = pl.num_programs(0) * (BQ // STEP) - steps * (BK // STEP)
    bounds_ref[block, 0] = jnp.minimum(low, room)
    bounds_ref[block, 1] = steps
    unit, _ = normalized(x_ref[...].astype(F32))
    xn = (unit * gain_ref[0:1, :].astype(F32) + shift_ref[0:1, :].astype(F32)).astype(BF16)
    unit_ref[...] = unit.astype(BF16)
    for item, (rows_ref, cols_ref) in enumerate(((q_ref, qt_ref), (k_ref, kt_ref), (None, vt_ref))):
        cols_ref[...] = dot_nt(full_ref[item], xn).astype(BF16)
        if rows_ref is not None:
            full = dot_nt(xn, full_ref[item]).astype(BF16)
            for head in range(heads):
                rows_ref[head] = full[:, head * HD : (head + 1) * HD]


def project(lens, tokens, gains, shifts, weights, depth):
    count, dim = tokens.shape
    width = weights.shape[2]
    heads = width // HD
    blocks = count // BQ
    per_head = pl.BlockSpec((heads, BQ, HD), lambda i: (0, i, 0))
    turned = pl.BlockSpec((width, BQ), lambda i: (0, i))
    fixed2 = pl.BlockSpec((2, dim), lambda i: (0, 0))
    return pl.pallas_call(
        project_kernel,
        grid=(blocks,),
        in_specs=[
            pl.BlockSpec(memory_space=pltpu.SMEM),
            pl.BlockSpec((BQ, dim), lambda i: (i, 0)),
            fixed2,
            fixed2,
            pl.BlockSpec(weights.shape, lambda i: (0, 0, 0, 0)),
        ],
        out_specs=[
            pl.BlockSpec((BQ, dim), lambda i: (i, 0)),
            per_head,
            per_head,
            turned,
            turned,
            turned,
            pl.BlockSpec((BQ, 128), lambda i: (i, 0)),
            pl.BlockSpec((8, BQ), lambda i: (0, i)),
            pl.BlockSpec(memory_space=pltpu.SMEM),
            pl.BlockSpec((3, width, dim), lambda i: (0, 0, 0)),
            pl.BlockSpec((depth, width, dim), lambda i: (0, 0, 0)),
        ],
        out_shape=[
            jax.ShapeDtypeStruct((count, dim), BF16),
            jax.ShapeDtypeStruct((heads, count, HD), BF16),
            jax.ShapeDtypeStruct((heads, count, HD), BF16),
            jax.ShapeDtypeStruct((width, count), BF16),
            jax.ShapeDtypeStruct((width, count), BF16),
            jax.ShapeDtypeStruct((width, count), BF16),
            jax.ShapeDtypeStruct((count, 128), jnp.int32),
            jax.ShapeDtypeStruct((8, count), jnp.int32),
            jax.ShapeDtypeStruct((blocks, 2), jnp.int32),
            jax.ShapeDtypeStruct((3, width, dim), BF16),
            jax.ShapeDtypeStruct((depth, width, dim), BF16),
        ],
        compiler_params=pltpu.CompilerParams(vmem_limit_bytes=VMEM_LIMIT),
        cost_estimate=COST,
        name="project",
    )(lens, tokens, gains, shifts, weights)


def spread_lanes(column, width):
    return jnp.concatenate([column] * (width // 128), axis=1) if width > 128 else column


def spot_of(layer, item, size):
    return pl.ds(pl.multiple_of((layer[0] ^ item) * size, 128), size)


def attend_kernel(
    first, heads, parts, layer, bounds, segc_ref, segr_ref, k_ref, qt_ref, vt_ref, *refs
):
    part_refs, (ot_ref, lse_ref) = refs[:parts], refs[parts:]
    count = segc_ref.shape[0]
    factor = SCALE * LOG2E

    def q_block(block, _):
        start = pl.multiple_of(block * BQ, BQ)
        seg_q = segr_ref[0:1, pl.ds(start, BQ)]
        queries = [
            qt_ref[(first + h) * HD : (first + h + 1) * HD, pl.ds(start, BQ)] for h in range(heads)
        ]

        def k_block(item, carry):
            at = pl.multiple_of(bounds[block, 0] * STEP + item * BK, STEP)
            allowed = spread_lanes(segc_ref[pl.ds(at, BK), :], BQ) == seg_q
            out = []
            scores = [dot(k_ref[first + h, pl.ds(at, BK), :], queries[h]) for h in range(heads)]
            scores = [jnp.where(allowed, value, -1e30) for value in scores]
            fresh = [
                jnp.maximum(carry[h][0], jnp.max(scores[h], axis=0, keepdims=True))
                for h in range(heads)
            ]
            expd = [jnp.exp2((scores[h] - fresh[h]) * factor) for h in range(heads)]
            for h in range(heads):
                top, total, acc = carry[h]
                fade = jnp.exp2((top - fresh[h]) * factor)
                total = total * fade + jnp.sum(expd[h], axis=0, keepdims=True)
                rows = vt_ref[(first + h) * HD : (first + h + 1) * HD, pl.ds(at, BK)]
                acc = acc * fade + dot(rows, expd[h].astype(BF16))
                out.append((fresh[h], total, acc))
            return tuple(out)

        empty = (
            jnp.full((1, BQ), -1e30, F32),
            jnp.zeros((1, BQ), F32),
            jnp.zeros((HD, BQ), F32),
        )
        done = lax.fori_loop(0, bounds[block, 1], k_block, (empty,) * heads)
        for h in range(heads):
            top, total, acc = done[h]
            ot_ref[h * HD : (h + 1) * HD, pl.ds(start, BQ)] = acc / total
            lse_ref[h : h + 1, pl.ds(start, BQ)] = top * factor + jnp.log(total) * LOG2E
        return 0

    lax.fori_loop(0, count // BQ, q_block, 0)
    size = count // parts
    for part in range(parts):
        part_refs[part][...] = ot_ref[:, spot_of(layer, part, size)].astype(BF16)


def attend(first, heads, parts, layer, tables, k_rows, q_cols, v_cols):
    segc, segr, bounds = tables
    count = segc.shape[0]
    out = pl.pallas_call(
        partial(attend_kernel, first, heads, parts),
        in_specs=[pl.BlockSpec(memory_space=pltpu.SMEM)] * 2 + [vmem()] * 5,
        out_specs=[vmem()] * (parts + 2),
        out_shape=[jax.ShapeDtypeStruct((heads * HD, count // parts), BF16)] * parts
        + [
            jax.ShapeDtypeStruct((heads * HD, count), F32),
            jax.ShapeDtypeStruct((8, count), F32),
        ],
        compiler_params=pltpu.CompilerParams(vmem_limit_bytes=VMEM_LIMIT),
        cost_estimate=COST,
        name=f"attend_{first}",
    )(layer, bounds, segc, segr, k_rows, q_cols, v_cols)
    return out[:parts], out[parts], out[parts + 1]


def attend_back_kernel(
    first, heads, parts, layer, bounds, segc_ref, segr_ref,
    q_ref, k_ref, qt_ref, kt_ref, vt_ref, ot_ref, lse_ref, *refs,
):
    part_refs, out_refs, refs = refs[:parts], refs[parts : 2 * parts], refs[2 * parts :]
    flat_ref, dot_ref, do_ref, stat_ref, dq_ref, dqt_ref, dkt_ref, dvt_ref = refs
    count = segc_ref.shape[0]
    factor = SCALE * LOG2E
    size = count // parts
    for part in range(parts):
        value = part_refs[part][first * HD : (first + heads) * HD, :]
        dot_ref[:, spot_of(layer, part, size)] = value
        for h in range(heads):
            do_ref[h, spot_of(layer, part, size), :] = value[h * HD : (h + 1) * HD, :].T
    dkt_ref[...] = jnp.zeros_like(dkt_ref)
    dvt_ref[...] = jnp.zeros_like(dvt_ref)

    def q_block(block, _):
        start = pl.multiple_of(block * BQ, BQ)
        spot = pl.ds(start, BQ)
        stats = [lse_ref[0:heads, spot]]
        for h in range(heads):
            lane = slice(h * HD, (h + 1) * HD)
            stats.append(
                jnp.sum(dot_ref[lane, spot].astype(F32) * ot_ref[lane, spot], axis=0, keepdims=True)
            )
        stats.append(jnp.zeros((8 - 2 * heads, BQ), F32)) if heads < 4 else None
        turned = jnp.concatenate(stats, axis=0).T
        for h in range(2 * heads):
            stat_ref[h] = jnp.broadcast_to(turned[:, h : h + 1], (BQ, 128))
        dq_ref[...] = jnp.zeros_like(dq_ref)
        seg_q = spread_lanes(segc_ref[spot, :], BK)

        def k_block(item, _):
            at = pl.multiple_of(bounds[block, 0] * STEP + item * BK, STEP)
            here = pl.ds(at, BK)
            allowed = seg_q == segr_ref[0:1, here]
            lanes = [slice(h * HD, (h + 1) * HD) for h in range(heads)]
            owns = [slice((first + h) * HD, (first + h + 1) * HD) for h in range(heads)]
            scores = [dot(q_ref[first + h, spot, :], kt_ref[owns[h], here]) for h in range(heads)]
            dprob = [dot(do_ref[h, spot, :], vt_ref[owns[h], here]) for h in range(heads)]
            prob = [
                jnp.where(
                    allowed, jnp.exp2(scores[h] * factor - spread_lanes(stat_ref[h], BK)), 0.0
                )
                for h in range(heads)
            ]
            dscore = [
                (prob[h] * (dprob[h] - spread_lanes(stat_ref[heads + h], BK))).astype(BF16)
                for h in range(heads)
            ]
            for h in range(heads):
                dvt_ref[lanes[h], here] += dot(dot_ref[lanes[h], spot], prob[h].astype(BF16))
                dkt_ref[lanes[h], here] += dot(qt_ref[owns[h], spot], dscore[h])
                dq_ref[h] += dot(dscore[h], k_ref[first + h, here, :])
            return 0

        lax.fori_loop(0, bounds[block, 1], k_block, 0)
        for h in range(heads):
            dqt_ref[h * HD : (h + 1) * HD, spot] = dq_ref[h].T * SCALE
        return 0

    lax.fori_loop(0, count // BQ, q_block, 0)
    width = heads * HD
    for item, (source, scale) in enumerate(((dqt_ref, 1.0), (dkt_ref, SCALE), (dvt_ref, 1.0))):
        value = source[...] if scale == 1.0 else source[...] * scale
        value = value.astype(BF16)
        flat_ref[item * width : (item + 1) * width, :] = value
    for part in range(parts):
        out_refs[part][...] = flat_ref[:, spot_of(layer, part, size)]


def attend_back(first, heads, layer, tables, q_rows, k_rows, q_cols, k_cols, v_cols, out, lse, dout):
    segc, segr, bounds = tables
    count = segc.shape[0]
    parts = len(dout)
    width = heads * HD
    result = pl.pallas_call(
        partial(attend_back_kernel, first, heads, parts),
        in_specs=[pl.BlockSpec(memory_space=pltpu.SMEM)] * 2 + [vmem()] * (9 + parts),
        out_specs=[vmem()] * (parts + 1),
        out_shape=[jax.ShapeDtypeStruct((3 * width, count // parts), BF16)] * parts
        + [jax.ShapeDtypeStruct((3 * width, count), BF16)],
        scratch_shapes=[
            pltpu.VMEM((width, count), BF16),
            pltpu.VMEM((heads, count, HD), BF16),
            pltpu.VMEM((2 * heads, BQ, 128), F32),
            pltpu.VMEM((heads, BQ, HD), F32),
            pltpu.VMEM((width, count), F32),
            pltpu.VMEM((width, count), F32),
            pltpu.VMEM((width, count), F32),
        ],
        compiler_params=pltpu.CompilerParams(vmem_limit_bytes=VMEM_LIMIT),
        cost_estimate=COST,
        name=f"attend_back_{first}",
    )(layer, bounds, segc, segr, q_rows, k_rows, q_cols, k_cols, v_cols, out, lse, *dout)
    return result[:parts], result[parts]


def mix_kernel(parts, layer, *refs):
    ot_refs, w_ref, refs = refs[:parts], refs[parts], refs[parts + 1 :]
    x_ref, gain_ref, shift_ref, x2_ref, xn_ref, ot_ref = refs
    middle = x_ref[...].astype(F32)
    for part in range(parts):
        value = ot_refs[part][...]
        ot_ref[layer[0] ^ part] = value
        middle = middle + dot(value.T, w_ref[layer[0] ^ part])
    x2_ref[...] = middle
    unit, _ = normalized(middle)
    xn_ref[...] = (unit * gain_ref[1:2, :].astype(F32) + shift_ref[1:2, :].astype(F32)).astype(BF16)


def mix(layer, ot, w_out, rows, gains, shifts):
    count, dim = rows.shape
    parts = len(ot)
    return pl.pallas_call(
        partial(mix_kernel, parts),
        in_specs=[pl.BlockSpec(memory_space=pltpu.SMEM)] + [vmem()] * (parts + 4),
        out_specs=[vmem()] * 3,
        out_shape=[
            jax.ShapeDtypeStruct((count, dim), F32),
            jax.ShapeDtypeStruct((count, dim), BF16),
            jax.ShapeDtypeStruct((parts,) + ot[0].shape, BF16),
        ],
        compiler_params=pltpu.CompilerParams(vmem_limit_bytes=VMEM_LIMIT),
        cost_estimate=COST,
        name="mix",
    )(layer, *ot, w_out, rows, gains, shifts)


ROWS = 256


def ffn_kernel(*refs):
    xn_parts, dy_parts, w_ref = refs[:2], refs[2:4], refs[4]
    y_out, dx_out, y_far, dx_far, g_ref, du_ref = refs[5:11]
    y_ref, dx_ref, xn_ref, dy_ref = refs[11:]
    item = pl.program_id(0)
    mine = xn_parts[0].shape[0]
    count, hidden = g_ref.shape

    @pl.when(item == 0)
    def _():
        for part in range(2):
            xn_ref[part * mine : (part + 1) * mine, :] = xn_parts[part][...]
            dy_ref[part * mine : (part + 1) * mine, :] = dy_parts[part][...]
        y_ref[...] = jnp.zeros_like(y_ref)
        dx_ref[...] = jnp.zeros_like(dx_ref)

    w_in = w_ref.at[:, :hidden]
    w_down = w_ref.at[:, hidden:]
    for first in range(0, count, ROWS):
        rows = slice(first, first + ROWS)
        u = dot(xn_ref[rows, :], w_in[...])
        dg = dot(dy_ref[rows, :], w_down[...])
        half = 0.5 + 0.5 * lax.erf(u * 0.7071067811865476)
        slope = half + u * (jnp.exp2(u * u * (-0.5 * LOG2E)) * 0.3989422804014327)
        g = (u * half).astype(BF16)
        du = (dg * slope).astype(BF16)
        g_ref[rows, :] = g
        du_ref[rows, :] = du
        y_ref[rows, :] += dot_nt(g, w_down[...])
        dx_ref[rows, :] += dot_nt(du, w_in[...])

    @pl.when(item == pl.num_programs(0) - 1)
    def _():
        y_out[...] = y_ref[:mine, :]
        dx_out[...] = dx_ref[:mine, :]
        y_far[...] = y_ref[mine:, :].astype(BF16)
        dx_far[...] = dx_ref[mine:, :].astype(BF16)


def ffn(xn, dy, weights):
    mine, dim = xn[0].shape
    count = 2 * mine
    blocks = weights.shape[0] // dim
    hidden = weights.shape[1] // 2
    whole = pl.BlockSpec((mine, dim), lambda i: (0, 0))
    act = pl.BlockSpec((count, hidden), lambda i: (0, i))
    return pl.pallas_call(
        ffn_kernel,
        grid=(blocks,),
        in_specs=[whole] * 4 + [pl.BlockSpec((dim, 2 * hidden), lambda i: (i, 0))],
        out_specs=[whole] * 4 + [act] * 2,
        out_shape=[jax.ShapeDtypeStruct((mine, dim), F32)] * 2
        + [jax.ShapeDtypeStruct((mine, dim), BF16)] * 2
        + [jax.ShapeDtypeStruct((count, blocks * hidden), BF16)] * 2,
        scratch_shapes=[pltpu.VMEM((count, dim), F32)] * 2 + [pltpu.VMEM((count, dim), BF16)] * 2,
        compiler_params=pltpu.CompilerParams(vmem_limit_bytes=VMEM_LIMIT),
        cost_estimate=COST,
        name="ffn",
    )(*xn, *dy, weights)


def outer_kernel(sides, _, *refs):
    xn_parts, dy_parts = refs[: 2 * sides], refs[2 * sides : 4 * sides]
    g_refs, du_refs = refs[4 * sides : 5 * sides], refs[5 * sides : 6 * sides]
    grad_ref, xnt_ref, dyt_ref = refs[6 * sides :]
    mine = xn_parts[0].shape[0]
    hidden = g_refs[0].shape[1]

    @pl.when(pl.program_id(0) == 0)
    def _():
        for part in range(2 * sides):
            xnt_ref[:, part * mine : (part + 1) * mine] = xn_parts[part][...].T
            dyt_ref[:, part * mine : (part + 1) * mine] = dy_parts[part][...].T

    for at, turned, sources in ((0, xnt_ref, du_refs), (hidden, dyt_ref, g_refs)):
        total = None
        for side in range(sides):
            cut = slice(2 * side * mine, 2 * (side + 1) * mine)
            term = dot(turned[:, cut], sources[side][...])
            total = term if total is None else total + term
        grad_ref[0, :, at : at + hidden] = total.astype(BF16)


def outer(base, xn, dy, g, du, hidden):
    sides = len(g)
    mine, dim = xn[0].shape
    count = 2 * mine
    blocks = g[0].shape[1] // hidden
    whole = pl.BlockSpec((mine, dim), lambda i, base: (0, 0))
    act = pl.BlockSpec((count, hidden), lambda i, base: (0, i ^ base[0]))
    return pl.pallas_call(
        partial(outer_kernel, sides),
        grid_spec=pltpu.PrefetchScalarGridSpec(
            num_scalar_prefetch=1,
            grid=(blocks,),
            in_specs=[whole] * (4 * sides) + [act] * (2 * sides),
            out_specs=pl.BlockSpec((1, dim, 2 * hidden), lambda i, base: (i, 0, 0)),
            scratch_shapes=[pltpu.VMEM((dim, sides * count), BF16)] * 2,
        ),
        out_shape=jax.ShapeDtypeStruct((blocks, dim, 2 * hidden), BF16),
        compiler_params=pltpu.CompilerParams(vmem_limit_bytes=VMEM_LIMIT),
        cost_estimate=COST,
        name="outer",
    )(base, *xn, *dy, *g, *du)


def turn_kernel(layer, w_ref, *refs):
    x2_ref, dx_ref, core_ref, near_ref, dy_ref, ot_ref, gain_ref = refs[:7]
    dx2_ref, gout_ref, sums_ref = refs[7:10]
    dot_refs = refs[10:]
    middle = x2_ref[...]
    grad = dx_ref[...] + core_ref[...].astype(F32) + near_ref[...].astype(F32)
    back, prod = norm_backward(middle, gain_ref[1:2, :].astype(F32), grad)
    dx2 = dy_ref[...].astype(F32) + back
    dx2_ref[...] = dx2
    sums_ref[...] = jnp.concatenate(
        [
            jnp.sum(prod, axis=0, keepdims=True),
            jnp.sum(grad, axis=0, keepdims=True),
            jnp.zeros((6, grad.shape[1]), F32),
        ],
        axis=0,
    )
    low = dx2.astype(BF16)
    across = low.T
    width = ot_ref.shape[1]
    for part in range(w_ref.shape[0]):
        dot_refs[part][...] = dot(w_ref[layer[0] ^ part], across).astype(BF16)
        gout_ref[:, part * width : (part + 1) * width] = dot_nt(across, ot_ref[part]).astype(BF16)


def turn(layer, w_out, x2, dx, core, near, dy, ot, gains):
    count, dim = x2.shape
    parts = w_out.shape[0]
    out = pl.pallas_call(
        turn_kernel,
        in_specs=[pl.BlockSpec(memory_space=pltpu.SMEM)] + [vmem()] * 8,
        out_specs=[vmem()] * (parts + 3),
        out_shape=[
            jax.ShapeDtypeStruct((count, dim), F32),
            jax.ShapeDtypeStruct((dim, dim), BF16),
            jax.ShapeDtypeStruct((8, dim), F32),
        ]
        + [jax.ShapeDtypeStruct(ot.shape[1:], BF16)] * parts,
        compiler_params=pltpu.CompilerParams(vmem_limit_bytes=VMEM_LIMIT),
        cost_estimate=COST,
        name="turn",
    )(layer, w_out, x2, dx, core, near, dy, ot, gains)
    return *out[:3], out[3:]


def finish_kernel(parts, layer, *refs):
    part_refs, refs = refs[:parts], refs[parts:]
    w_ref, x_ref, dx2_ref, gain_ref, out_ref = refs
    width = w_ref.shape[2]
    grad = None
    for part in range(parts):
        for item in range(3):
            value = part_refs[part][item * width : (item + 1) * width, :]
            term = dot(value.T, w_ref[layer[0] ^ part, item])
            grad = term if grad is None else grad + term
    back, _ = norm_backward(x_ref[...].astype(F32), gain_ref[0:1, :].astype(F32), grad)
    out_ref[...] = (dx2_ref[...] + back).astype(BF16)


def finish(layer, parts, w_qkv, rows, dx2, gains):
    count, dim = rows.shape
    return pl.pallas_call(
        partial(finish_kernel, len(parts)),
        in_specs=[pl.BlockSpec(memory_space=pltpu.SMEM)] + [vmem()] * (len(parts) + 4),
        out_specs=vmem(),
        out_shape=jax.ShapeDtypeStruct((count, dim), BF16),
        compiler_params=pltpu.CompilerParams(vmem_limit_bytes=VMEM_LIMIT),
        cost_estimate=COST,
        name="finish",
    )(layer, *parts, w_qkv, rows, dx2, gains)


def small_kernel(flat_ref, unit_ref, w_ref, gain_ref, shift_ref, gout_ref, sums_ref, out_ref):
    dim = unit_ref.shape[1]
    inner = dot(flat_ref[...], unit_ref[...])
    sums = jnp.sum(flat_ref[...].astype(F32), axis=1, keepdims=True)
    grad = inner * gain_ref[0:1, :].astype(F32) + sums * shift_ref[0:1, :].astype(F32)
    width = w_ref.shape[1]
    gain = jnp.zeros((1, dim), F32)
    shift = jnp.zeros((1, dim), F32)
    for item in range(3):
        rows = slice(item * width, (item + 1) * width)
        w = w_ref[item].astype(F32)
        gain = gain + jnp.sum(w * inner[rows, :], axis=0, keepdims=True)
        shift = shift + jnp.sum(w * sums[rows, :], axis=0, keepdims=True)
    side = 3 * width
    out_ref[:, :dim] = gout_ref[...]
    out_ref[:, dim : dim + side] = grad.T.astype(BF16)
    sums = jnp.concatenate([gain, sums_ref[0:1, :], shift, sums_ref[1:2, :]], axis=0)
    sums = jnp.concatenate([sums, jnp.zeros((out_ref.shape[1] - dim - side - 4, dim), F32)], axis=0)
    out_ref[:, dim + side :] = sums.T.astype(BF16)


def small(flat, unit, w_qkv, gains, shifts, grad_out, sums):
    side, dim = flat.shape[0], unit.shape[1]
    total = -(-(dim + side + 8) // 128) * 128
    return pl.pallas_call(
        small_kernel,
        in_specs=[vmem()] * 7,
        out_specs=vmem(),
        out_shape=jax.ShapeDtypeStruct((dim, total), BF16),
        compiler_params=pltpu.CompilerParams(vmem_limit_bytes=VMEM_LIMIT),
        cost_estimate=COST,
        name="small",
    )(flat, unit, w_qkv, gains, shifts, grad_out, sums)


def collect_kernel(layer, *refs):
    parts, out_ref = refs[:-1], refs[-1]
    size = parts[0].shape[0]
    for item, part in enumerate(parts):
        out_ref[pl.ds(pl.multiple_of((layer[0] ^ item) * size, 128), size), :] = part[...]


def collect(layer, parts):
    size, dim = parts[0].shape
    return pl.pallas_call(
        collect_kernel,
        in_specs=[pl.BlockSpec(memory_space=pltpu.SMEM)] + [vmem()] * len(parts),
        out_specs=vmem(),
        out_shape=jax.ShapeDtypeStruct((size * len(parts), dim), parts[0].dtype),
        compiler_params=pltpu.CompilerParams(vmem_limit_bytes=VMEM_LIMIT),
        cost_estimate=COST,
        name="collect",
    )(layer, *parts)


WIDE = ("far", "near", "core")


def swap(value, axis):
    return lax.ppermute(value, axis, [(0, 1), (1, 0)])


def spread(parts):
    size = len(parts)
    return [parts[0]] + [
        lax.ppermute(parts[bit], "narrow", [(i, i ^ bit) for i in range(size)])
        for bit in range(1, size)
    ]


def exchange(value, axis):
    return lax.all_to_all(value, axis, 0, 0, tiled=True)


def after(value, *others):
    return lax.optimization_barrier((value,) + others)[0]


def add(*parts):
    return sum(part.astype(F32) for part in parts).astype(BF16)


def local(
    tokens, cotangent, seq_lens, norm_gains, norm_shifts, w_qkv, w_attn_out, w_ffn_in, w_ffn_down
):
    depth = lax.axis_size("narrow")
    across = lax.axis_size(WIDE)
    count, dim = tokens.shape
    mine = count // depth
    width = w_qkv.shape[2]
    cols = w_ffn_in.shape[1]
    heads = width // HD
    layer = lax.axis_index("narrow")
    layers = layer.astype(jnp.int32).reshape(1)

    pieces = lax.all_gather(
        jnp.concatenate([jnp.swapaxes(w_qkv, 1, 2), w_attn_out[None]], axis=0), WIDE, axis=0
    )
    weights = lax.all_gather(
        jnp.concatenate([w_ffn_in, w_ffn_down], axis=1), ("far", "narrow"), axis=0, tiled=True
    )
    group = max(1, dim // cols)
    shape = (-1, group, dim, 2, cols)
    if group > 1:
        weights = weights.reshape(shape).transpose(0, 2, 3, 1, 4).reshape(-1, 2 * group * cols)
    rows = lax.dynamic_slice_in_dim(tokens, layer * mine, mine, 0)
    dy = lax.dynamic_slice_in_dim(cotangent, layer * mine, mine, 0)
    dy_near = swap(dy, "near")
    dy_own = (dy, swap(dy, "core"))
    dy_far = (dy_near, swap(dy_near, "core"))

    unit, q_rows, k_rows, q_cols, k_cols, v_cols, *tables, w_proj, w_out = project(
        seq_lens, tokens, norm_gains, norm_shifts, pieces, depth
    )
    w_out = exchange(w_out, "narrow")
    parts, out, lse = attend(0, heads, depth, layers, tables, k_rows, q_cols, v_cols)
    x2, xn2, ot = mix(layers, spread(parts), w_out, rows, norm_gains, norm_shifts)
    xn_near = swap(xn2, "near")
    xn_own = (xn2, swap(xn2, "core"))
    w_proj_all = lax.all_gather(w_proj, "narrow", axis=0)

    y_a, dx_a, y_core, dx_core, g_a, du_a = ffn(xn_own, dy_own, weights)
    xn_near = after(xn_near, y_a)
    xn_far = (xn_near, swap(xn_near, "core"))
    y_b, dx_b, y_far, dx_far, g_b, du_b = ffn(xn_far, dy_far, weights)
    dx_core = swap(dx_core, "core")
    dx_near = swap(add(dx_b, swap(dx_far, "core")), "near")
    pair = lax.axis_size("far") == 2
    base = lax.axis_index("far") if pair else jnp.zeros((), jnp.int32)
    base = base.astype(jnp.int32).reshape(1)
    grads = outer(base, xn_own + xn_far, dy_own + dy_far, (g_a, g_b), (du_a, du_b), group * cols)
    dx2, grad_out, norm_two, dout = turn(
        layers, w_out, after(x2, grads), dx_a, dx_core, dx_near, dy, ot, norm_gains
    )
    dout = spread(dout)
    y_core, y_far = (swap(part, "core") for part in (y_core, y_far))
    y_near = swap(add(y_b, y_far), "near")
    out_mine = (x2 + y_a + y_core.astype(F32) + y_near.astype(F32)).astype(BF16)
    dout, out_mine = lax.optimization_barrier((dout, out_mine))
    layer_out = lax.all_gather(out_mine, "narrow", axis=0, tiled=True)
    back, flat_back = attend_back(
        0, heads, layers, tables, q_rows, k_rows, q_cols, k_cols, v_cols, out, lse, dout
    )
    if pair:
        back, far_grads = lax.optimization_barrier((back, swap(grads[1], "far")))
        total = add(after(grads[0], flat_back), far_grads)
    else:
        grads = grads.reshape(-1, dim, 2, group, cols).transpose(0, 3, 1, 2, 4)
        grads = grads.reshape(-1, dim, 2 * cols)
        total = lax.psum_scatter(grads, "far", scatter_dimension=0, tiled=False)
    total = lax.psum_scatter(total, "narrow", scatter_dimension=0, tiled=True).astype(F32)

    back = spread(back)
    in_mine = finish(layers, back, w_proj_all, rows, dx2, norm_gains)
    input_grad = lax.all_gather(in_mine, "narrow", axis=0, tiled=True)

    side = 3 * width
    part = dim // across
    rest = small(
        after(flat_back, in_mine), unit, w_proj, norm_gains, norm_shifts, grad_out, norm_two
    )
    rest = exchange(rest.reshape(across, part, -1), WIDE)
    rest = jnp.sum(rest.astype(F32), axis=0)
    gqkv = rest[:, dim : dim + side].reshape(part, 3, width).transpose(1, 0, 2)
    gout = rest[:, :dim].astype(BF16).reshape(part, depth, width).transpose(1, 0, 2)
    norms = rest[:, dim + side : dim + side + 4].astype(BF16)
    gout = jnp.concatenate([gout, jnp.broadcast_to(norms, (depth, part, 4))], axis=2)
    gout = jnp.sum(exchange(gout, "narrow").astype(F32), axis=0).T
    gout, norms = gout[:width], gout[width:]
    return (
        layer_out,
        input_grad,
        norms[:2],
        norms[2:],
        gqkv,
        gout,
        total[:, :cols],
        total[:, cols:],
    )


def solution(mesh):
    depth, across = mesh.shape["narrow"], mesh.shape["wide"]
    fine = jax.sharding.Mesh(
        mesh.devices.reshape(depth, across // 4, 2, 2), ("narrow", "far", "near", "core")
    )
    return jax.shard_map(
        local,
        mesh=fine,
        in_specs=(
            P(WIDE, None),
            P(WIDE, None),
            P(WIDE, None),
            P(),
            P(),
            P(None, WIDE, "narrow"),
            P("narrow", WIDE),
            P("narrow", WIDE),
            P("narrow", WIDE),
        ),
        out_specs=(
            P(WIDE, None),
            P(WIDE, None),
            P(None, WIDE),
            P(None, WIDE),
            P(None, WIDE, "narrow"),
            P("narrow", WIDE),
            P("narrow", WIDE),
            P("narrow", WIDE),
        ),
        check_vma=False,
    )
```

```python
from functools import partial

import jax
import jax.numpy as jnp
from jax import lax
from jax.experimental import pallas as pl
from jax.experimental.pallas import tpu as pltpu
from jax.sharding import PartitionSpec as P

HD = 32
EPS = 1e-05
LOG2E = 1.4426950408889634
SCALE = HD ** (-0.5)
BQ = 256
BK = 256
STEP = 256
STEPS = 3
BF16 = jnp.bfloat16
F32 = jnp.float32
VMEM_LIMIT = 56 * 1024 * 1024
COST = pl.CostEstimate(flops=1000000, bytes_accessed=100000, transcendentals=0)


def vmem(*shape):
    return pl.BlockSpec(shape, None) if shape else pl.BlockSpec(memory_space=pltpu.VMEM)


def dot(a, b):
    return jnp.dot(a, b, preferred_element_type=F32)


def dot_nt(a, b):
    return lax.dot_general(a, b, (((1,), (1,)), ((), ())), preferred_element_type=F32)


def normalized(rows):
    center = rows - jnp.mean(rows, axis=-1, keepdims=True)
    spread = jnp.mean(center * center, axis=-1, keepdims=True)
    inverse = lax.rsqrt(spread + EPS)
    return center * inverse, inverse


def norm_backward(rows, gain, grad):
    unit, inverse = normalized(rows)
    scaled = grad * gain
    inner = scaled - jnp.mean(scaled, axis=-1, keepdims=True)
    inner = inner - unit * jnp.mean(scaled * unit, axis=-1, keepdims=True)
    return inverse * inner, grad * unit


def project_kernel(
    lens, x_ref, gain_ref, shift_ref, w_ref,
    q_ref, k_ref, qt_ref, kt_ref, vt_ref, seg_ref, bounds_ref, full_ref, out_ref,
):
    across, kinds, _, narrow = w_ref.shape

    @pl.when(pl.program_id(0) == 0)
    def _():
        for part in range(across):
            spot = slice(part * narrow, (part + 1) * narrow)
            for item in range(kinds - 1):
                full_ref[item, :, spot] = w_ref[part, item]
            for copy in range(out_ref.shape[0]):
                out_ref[copy, :, spot] = w_ref[part, kinds - 1]

    size = x_ref.shape[0]
    first = pl.program_id(0) * size
    tiles = size // BQ
    end = jnp.int32(0)
    low = [jnp.int32(0)] * tiles
    high = [jnp.int32(0) + pl.num_programs(0) * size] * tiles
    cols = first + lax.broadcasted_iota(jnp.int32, seg_ref.shape, 1)
    segment = jnp.zeros(seg_ref.shape, jnp.int32)
    for item in range(lens.shape[1]):
        end = end + lens[0, item]
        for tile in range(tiles):
            start = first + tile * BQ
            low[tile] = jnp.where(end <= start, end, low[tile])
            later = (end > start + (BQ - 1)) & (end < high[tile])
            high[tile] = jnp.where(later, end, high[tile])
        segment = segment + (cols >= end).astype(jnp.int32)
    seg_ref[...] = segment.astype(F32)
    for tile in range(tiles):
        lowest = lax.div(low[tile], jnp.int32(STEP))
        highest = lax.div(high[tile] + (STEP - 1), jnp.int32(STEP))
        steps = lax.div((highest - lowest) * STEP + (BK - 1), jnp.int32(BK))
        room = pl.num_programs(0) * (size // STEP) - steps * (BK // STEP)
        block = pl.program_id(0) * tiles + tile
        bounds_ref[block, 0] = jnp.minimum(lowest, room)
        bounds_ref[block, 1] = steps
    unit, _ = normalized(x_ref[...].astype(F32))
    xn = (unit * gain_ref[0:1, :].astype(F32) + shift_ref[0:1, :].astype(F32)).astype(BF16)
    for item, (rows_ref, cols_ref) in enumerate(((q_ref, qt_ref), (k_ref, kt_ref), (None, vt_ref))):
        cols_ref[...] = dot_nt(full_ref[item], xn).astype(BF16)
        if rows_ref is not None:
            full = dot_nt(xn, full_ref[item]).astype(BF16)
            for head in range(q_ref.shape[0]):
                rows_ref[head] = full[:, head * HD : (head + 1) * HD]


def project(lens, tokens, gains, shifts, weights, depth):
    count, dim = tokens.shape
    width = weights.shape[2]
    blocks = count // BQ
    size = count // STEPS
    heads = width // HD
    per_head = pl.BlockSpec((heads, size, HD), lambda i: (0, i, 0))
    turned = pl.BlockSpec((width, size), lambda i: (0, i))
    fixed2 = pl.BlockSpec((2, dim), lambda i: (0, 0))
    return pl.pallas_call(
        project_kernel,
        grid=(STEPS,),
        in_specs=[
            pl.BlockSpec(memory_space=pltpu.SMEM),
            pl.BlockSpec((size, dim), lambda i: (i, 0)),
            fixed2,
            fixed2,
            pl.BlockSpec(weights.shape, lambda i: (0, 0, 0, 0)),
        ],
        out_specs=[
            per_head,
            per_head,
            turned,
            turned,
            turned,
            pl.BlockSpec((8, size), lambda i: (0, i)),
            pl.BlockSpec(memory_space=pltpu.SMEM),
            pl.BlockSpec((3, width, dim), lambda i: (0, 0, 0)),
            pl.BlockSpec((depth, width, dim), lambda i: (0, 0, 0)),
        ],
        out_shape=[
            jax.ShapeDtypeStruct((heads, count, HD), BF16),
            jax.ShapeDtypeStruct((heads, count, HD), BF16),
            jax.ShapeDtypeStruct((width, count), BF16),
            jax.ShapeDtypeStruct((width, count), BF16),
            jax.ShapeDtypeStruct((width, count), BF16),
            jax.ShapeDtypeStruct((8, count), F32),
            jax.ShapeDtypeStruct((blocks, 2), jnp.int32),
            jax.ShapeDtypeStruct((3, width, dim), BF16),
            jax.ShapeDtypeStruct((depth, width, dim), BF16),
        ],
        compiler_params=pltpu.CompilerParams(vmem_limit_bytes=VMEM_LIMIT),
        cost_estimate=COST,
        name="project",
    )(lens, tokens, gains, shifts, weights)


def spread_lanes(column, width):
    return jnp.concatenate([column] * (width // 128), axis=1) if width > 128 else column


def spot_of(layer, item, size):
    return pl.ds(pl.multiple_of((layer[0] ^ item) * size, 128), size)


def column_of(row_ref, column_ref):
    for start in range(0, column_ref.shape[0], BK):
        turned = row_ref[:, start : start + BK].T
        column_ref[start : start + BK, :] = jnp.broadcast_to(turned[:, 0:1], (BK, 128))


def attend_kernel(
    first, heads, parts, layer, bounds, segr_ref, k_ref, qt_ref, vt_ref, *refs
):
    part_refs, (ot_ref, lse_ref, segc_ref) = refs[:parts], refs[parts:]
    count = segc_ref.shape[0]
    column_of(segr_ref, segc_ref)
    factor = SCALE * LOG2E

    def q_block(block, _):
        start = pl.multiple_of(block * BQ, BQ)
        seg_q = segr_ref[0:1, pl.ds(start, BQ)]
        queries = [
            qt_ref[(first + h) * HD : (first + h + 1) * HD, pl.ds(start, BQ)] for h in range(heads)
        ]

        def k_block(item, carry):
            at = pl.multiple_of(bounds[block, 0] * STEP + item * BK, STEP)
            allowed = spread_lanes(segc_ref[pl.ds(at, BK), :], BQ) == seg_q
            out = []
            scores = [dot(k_ref[first + h, pl.ds(at, BK), :], queries[h]) for h in range(heads)]
            scores = [jnp.where(allowed, value, -1e30) for value in scores]
            fresh = [
                jnp.maximum(carry[h][0], jnp.max(scores[h], axis=0, keepdims=True))
                for h in range(heads)
            ]
            expd = [jnp.exp2((scores[h] - fresh[h]) * factor) for h in range(heads)]
            for h in range(heads):
                top, total, acc = carry[h]
                fade = jnp.exp2((top - fresh[h]) * factor)
                total = total * fade + jnp.sum(expd[h], axis=0, keepdims=True)
                rows = vt_ref[(first + h) * HD : (first + h + 1) * HD, pl.ds(at, BK)]
                acc = acc * fade + dot(rows, expd[h].astype(BF16))
                out.append((fresh[h], total, acc))
            return tuple(out)

        empty = (
            jnp.full((1, BQ), -1e30, F32),
            jnp.zeros((1, BQ), F32),
            jnp.zeros((HD, BQ), F32),
        )
        done = lax.fori_loop(0, bounds[block, 1], k_block, (empty,) * heads)
        for h in range(heads):
            top, total, acc = done[h]
            ot_ref[h * HD : (h + 1) * HD, pl.ds(start, BQ)] = (acc / total).astype(BF16)
            lse_ref[h : h + 1, pl.ds(start, BQ)] = top * factor + jnp.log(total) * LOG2E
        return 0

    lax.fori_loop(0, count // BQ, q_block, 0)
    size = count // parts
    for part in range(parts):
        part_refs[part][...] = ot_ref[:, spot_of(layer, part, size)]


def attend(first, heads, parts, layer, tables, k_rows, q_cols, v_cols):
    segr, bounds = tables
    count = segr.shape[1]
    out = pl.pallas_call(
        partial(attend_kernel, first, heads, parts),
        in_specs=[pl.BlockSpec(memory_space=pltpu.SMEM)] * 2 + [vmem()] * 4,
        out_specs=[vmem()] * (parts + 2),
        out_shape=[jax.ShapeDtypeStruct((heads * HD, count // parts), BF16)] * parts
        + [
            jax.ShapeDtypeStruct((heads * HD, count), BF16),
            jax.ShapeDtypeStruct((8, count), F32),
        ],
        scratch_shapes=[pltpu.VMEM((count, 128), F32)],
        compiler_params=pltpu.CompilerParams(vmem_limit_bytes=VMEM_LIMIT),
        cost_estimate=COST,
        name=f"attend_{first}",
    )(layer, bounds, segr, k_rows, q_cols, v_cols)
    return out[:parts], out[parts], out[parts + 1]


def attend_back_kernel(
    first, heads, parts, layer, bounds, segr_ref,
    q_ref, k_ref, qt_ref, kt_ref, vt_ref, ot_ref, lse_ref, *refs,
):
    part_refs, out_refs, refs = refs[:parts], refs[parts : 2 * parts], refs[2 * parts :]
    flat_ref, segc_ref, dot_ref, do_ref, stat_ref, dq_ref, dqt_ref, dkt_ref, dvt_ref = refs
    count = segc_ref.shape[0]
    column_of(segr_ref, segc_ref)
    factor = SCALE * LOG2E
    size = count // parts
    for part in range(parts):
        value = part_refs[part][first * HD : (first + heads) * HD, :]
        dot_ref[:, spot_of(layer, part, size)] = value
        for h in range(heads):
            do_ref[h, spot_of(layer, part, size), :] = value[h * HD : (h + 1) * HD, :].T
    dkt_ref[...] = jnp.zeros_like(dkt_ref)
    dvt_ref[...] = jnp.zeros_like(dvt_ref)

    def q_block(block, _):
        start = pl.multiple_of(block * BQ, BQ)
        spot = pl.ds(start, BQ)
        stats = [lse_ref[0:heads, spot]]
        for h in range(heads):
            lane = slice(h * HD, (h + 1) * HD)
            stats.append(
                jnp.sum(
                    dot_ref[lane, spot].astype(F32) * ot_ref[lane, spot].astype(F32),
                    axis=0,
                    keepdims=True,
                )
            )
        stats.append(jnp.zeros((8 - 2 * heads, BQ), F32)) if heads < 4 else None
        turned = jnp.concatenate(stats, axis=0).T
        for h in range(2 * heads):
            stat_ref[h] = jnp.broadcast_to(turned[:, h : h + 1], (BQ, 128))
        dq_ref[...] = jnp.zeros_like(dq_ref)
        seg_q = spread_lanes(segc_ref[spot, :], BK)

        def k_block(item, _):
            at = pl.multiple_of(bounds[block, 0] * STEP + item * BK, STEP)
            here = pl.ds(at, BK)
            allowed = seg_q == segr_ref[0:1, here]
            lanes = [slice(h * HD, (h + 1) * HD) for h in range(heads)]
            owns = [slice((first + h) * HD, (first + h + 1) * HD) for h in range(heads)]
            scores = [dot(q_ref[first + h, spot, :], kt_ref[owns[h], here]) for h in range(heads)]
            dprob = [dot(do_ref[h, spot, :], vt_ref[owns[h], here]) for h in range(heads)]
            prob = [
                jnp.where(
                    allowed, jnp.exp2(scores[h] * factor - spread_lanes(stat_ref[h], BK)), 0.0
                )
                for h in range(heads)
            ]
            dscore = [
                (prob[h] * (dprob[h] - spread_lanes(stat_ref[heads + h], BK))).astype(BF16)
                for h in range(heads)
            ]
            for h in range(heads):
                dvt_ref[lanes[h], here] += dot(dot_ref[lanes[h], spot], prob[h].astype(BF16))
                dkt_ref[lanes[h], here] += dot(qt_ref[owns[h], spot], dscore[h])
                dq_ref[h] += dot(dscore[h], k_ref[first + h, here, :])
            return 0

        lax.fori_loop(0, bounds[block, 1], k_block, 0)
        for h in range(heads):
            dqt_ref[h * HD : (h + 1) * HD, spot] = dq_ref[h].T * SCALE
        return 0

    lax.fori_loop(0, count // BQ, q_block, 0)
    width = heads * HD
    for item, (source, scale) in enumerate(((dqt_ref, 1.0), (dkt_ref, SCALE), (dvt_ref, 1.0))):
        value = source[...] if scale == 1.0 else source[...] * scale
        value = value.astype(BF16)
        flat_ref[item * width : (item + 1) * width, :] = value
    for part in range(parts):
        out_refs[part][...] = flat_ref[:, spot_of(layer, part, size)]


def attend_back(first, heads, layer, tables, q_rows, k_rows, q_cols, k_cols, v_cols, out, lse, dout):
    segr, bounds = tables
    count = segr.shape[1]
    parts = len(dout)
    width = heads * HD
    result = pl.pallas_call(
        partial(attend_back_kernel, first, heads, parts),
        in_specs=[pl.BlockSpec(memory_space=pltpu.SMEM)] * 2 + [vmem()] * (8 + parts),
        out_specs=[vmem()] * (parts + 1),
        out_shape=[jax.ShapeDtypeStruct((3 * width, count // parts), BF16)] * parts
        + [jax.ShapeDtypeStruct((3 * width, count), BF16)],
        scratch_shapes=[
            pltpu.VMEM((count, 128), F32),
            pltpu.VMEM((width, count), BF16),
            pltpu.VMEM((heads, count, HD), BF16),
            pltpu.VMEM((2 * heads, BQ, 128), F32),
            pltpu.VMEM((heads, BQ, HD), F32),
            pltpu.VMEM((width, count), F32),
            pltpu.VMEM((width, count), F32),
            pltpu.VMEM((width, count), F32),
        ],
        compiler_params=pltpu.CompilerParams(vmem_limit_bytes=VMEM_LIMIT),
        cost_estimate=COST,
        name=f"attend_back_{first}",
    )(layer, bounds, segr, q_rows, k_rows, q_cols, k_cols, v_cols, out, lse, *dout)
    return result[:parts], result[parts]


def mix_kernel(parts, layer, *refs):
    ot_refs, w_ref, refs = refs[:parts], refs[parts], refs[parts + 1 :]
    x_ref, gain_ref, shift_ref, x2_ref, xn_ref, ot_ref = refs
    middle = x_ref[...].astype(F32)
    for part in range(parts):
        value = ot_refs[part][...]
        ot_ref[layer[0] ^ part] = value
        middle = middle + dot(value.T, w_ref[layer[0] ^ part])
    x2_ref[...] = middle
    unit, _ = normalized(middle)
    xn_ref[...] = (unit * gain_ref[1:2, :].astype(F32) + shift_ref[1:2, :].astype(F32)).astype(BF16)


def mix(layer, ot, w_out, rows, gains, shifts):
    count, dim = rows.shape
    parts = len(ot)
    return pl.pallas_call(
        partial(mix_kernel, parts),
        in_specs=[pl.BlockSpec(memory_space=pltpu.SMEM)] + [vmem()] * (parts + 4),
        out_specs=[vmem()] * 3,
        out_shape=[
            jax.ShapeDtypeStruct((count, dim), F32),
            jax.ShapeDtypeStruct((count, dim), BF16),
            jax.ShapeDtypeStruct((parts,) + ot[0].shape, BF16),
        ],
        compiler_params=pltpu.CompilerParams(vmem_limit_bytes=VMEM_LIMIT),
        cost_estimate=COST,
        name="mix",
    )(layer, *ot, w_out, rows, gains, shifts)


ROWS = 256


def ffn_kernel(*refs):
    xn_parts, dy_parts, w_ref = refs[:2], refs[2:4], refs[4]
    y_out, dx_out, y_far, dx_far, g_ref, du_ref = refs[5:11]
    y_ref, dx_ref, xn_ref, dy_ref = refs[11:]
    item = pl.program_id(0)
    mine = xn_parts[0].shape[0]
    count, hidden = g_ref.shape

    @pl.when(item == 0)
    def _():
        for part in range(2):
            xn_ref[part * mine : (part + 1) * mine, :] = xn_parts[part][...]
            dy_ref[part * mine : (part + 1) * mine, :] = dy_parts[part][...]
        y_ref[...] = jnp.zeros_like(y_ref)
        dx_ref[...] = jnp.zeros_like(dx_ref)

    w_in = w_ref.at[:, :hidden]
    w_down = w_ref.at[:, hidden:]
    for first in range(0, count, ROWS):
        rows = slice(first, first + ROWS)
        u = dot(xn_ref[rows, :], w_in[...])
        dg = dot(dy_ref[rows, :], w_down[...])
        half = 0.5 + 0.5 * lax.erf(u * 0.7071067811865476)
        slope = half + u * (jnp.exp2(u * u * (-0.5 * LOG2E)) * 0.3989422804014327)
        g = (u * half).astype(BF16)
        du = (dg * slope).astype(BF16)
        g_ref[rows, :] = g
        du_ref[rows, :] = du
        y_ref[rows, :] += dot_nt(g, w_down[...])
        dx_ref[rows, :] += dot_nt(du, w_in[...])

    @pl.when(item == pl.num_programs(0) - 1)
    def _():
        y_out[...] = y_ref[:mine, :].astype(BF16)
        dx_out[...] = dx_ref[:mine, :].astype(BF16)
        y_far[...] = y_ref[mine:, :].astype(BF16)
        dx_far[...] = dx_ref[mine:, :].astype(BF16)


def ffn(xn, dy, weights):
    mine, dim = xn[0].shape
    count = 2 * mine
    blocks = weights.shape[0] // dim
    hidden = weights.shape[1] // 2
    whole = pl.BlockSpec((mine, dim), lambda i: (0, 0))
    act = pl.BlockSpec((count, hidden), lambda i: (0, i))
    return pl.pallas_call(
        ffn_kernel,
        grid=(blocks,),
        in_specs=[whole] * 4 + [pl.BlockSpec((dim, 2 * hidden), lambda i: (i, 0))],
        out_specs=[whole] * 4 + [act] * 2,
        out_shape=[jax.ShapeDtypeStruct((mine, dim), BF16)] * 4
        + [jax.ShapeDtypeStruct((count, blocks * hidden), BF16)] * 2,
        scratch_shapes=[pltpu.VMEM((count, dim), F32)] * 2 + [pltpu.VMEM((count, dim), BF16)] * 2,
        compiler_params=pltpu.CompilerParams(vmem_limit_bytes=VMEM_LIMIT),
        cost_estimate=COST,
        name="ffn",
    )(*xn, *dy, weights)


def outer_kernel(sides, _, *refs):
    xn_parts, dy_parts = refs[: 2 * sides], refs[2 * sides : 4 * sides]
    g_refs, du_refs = refs[4 * sides : 5 * sides], refs[5 * sides : 6 * sides]
    grad_ref, xnt_ref, dyt_ref = refs[6 * sides :]
    mine = xn_parts[0].shape[0]
    hidden = g_refs[0].shape[1]

    @pl.when(pl.program_id(0) == 0)
    def _():
        for part in range(2 * sides):
            xnt_ref[:, part * mine : (part + 1) * mine] = xn_parts[part][...].T
            dyt_ref[:, part * mine : (part + 1) * mine] = dy_parts[part][...].T

    for at, turned, sources in ((0, xnt_ref, du_refs), (hidden, dyt_ref, g_refs)):
        total = None
        for side in range(sides):
            cut = slice(2 * side * mine, 2 * (side + 1) * mine)
            term = dot(turned[:, cut], sources[side][...])
            total = term if total is None else total + term
        grad_ref[0, :, at : at + hidden] = total.astype(BF16)


def outer(base, xn, dy, g, du, hidden):
    sides = len(g)
    mine, dim = xn[0].shape
    count = 2 * mine
    blocks = g[0].shape[1] // hidden
    whole = pl.BlockSpec((mine, dim), lambda i, base: (0, 0))
    act = pl.BlockSpec((count, hidden), lambda i, base: (0, i ^ base[0]))
    return pl.pallas_call(
        partial(outer_kernel, sides),
        grid_spec=pltpu.PrefetchScalarGridSpec(
            num_scalar_prefetch=1,
            grid=(blocks,),
            in_specs=[whole] * (4 * sides) + [act] * (2 * sides),
            out_specs=pl.BlockSpec((1, dim, 2 * hidden), lambda i, base: (i, 0, 0)),
            scratch_shapes=[pltpu.VMEM((dim, sides * count), BF16)] * 2,
        ),
        out_shape=jax.ShapeDtypeStruct((blocks, dim, 2 * hidden), BF16),
        compiler_params=pltpu.CompilerParams(vmem_limit_bytes=VMEM_LIMIT),
        cost_estimate=COST,
        name="outer",
    )(base, *xn, *dy, *g, *du)


def turn_kernel(layer, w_ref, *refs):
    x2_ref, dx_ref, core_ref, near_ref, dy_ref, ot_ref, gain_ref = refs[:7]
    dx2_ref, gout_ref, sums_ref = refs[7:10]
    dot_refs = refs[10:]
    middle = x2_ref[...]
    grad = dx_ref[...].astype(F32) + core_ref[...].astype(F32) + near_ref[...].astype(F32)
    back, prod = norm_backward(middle, gain_ref[1:2, :].astype(F32), grad)
    dx2 = dy_ref[...].astype(F32) + back
    dx2_ref[...] = dx2
    sums_ref[...] = jnp.concatenate(
        [
            jnp.sum(prod, axis=0, keepdims=True),
            jnp.sum(grad, axis=0, keepdims=True),
            jnp.zeros((6, grad.shape[1]), F32),
        ],
        axis=0,
    )
    low = dx2.astype(BF16)
    across = low.T
    width = ot_ref.shape[1]
    for part in range(w_ref.shape[0]):
        dot_refs[part][...] = dot(w_ref[layer[0] ^ part], across).astype(BF16)
        gout_ref[:, part * width : (part + 1) * width] = dot_nt(across, ot_ref[part]).astype(BF16)


def turn(layer, w_out, x2, dx, core, near, dy, ot, gains):
    count, dim = x2.shape
    parts = w_out.shape[0]
    out = pl.pallas_call(
        turn_kernel,
        in_specs=[pl.BlockSpec(memory_space=pltpu.SMEM)] + [vmem()] * 8,
        out_specs=[vmem()] * (parts + 3),
        out_shape=[
            jax.ShapeDtypeStruct((count, dim), F32),
            jax.ShapeDtypeStruct((dim, dim), BF16),
            jax.ShapeDtypeStruct((8, dim), F32),
        ]
        + [jax.ShapeDtypeStruct(ot.shape[1:], BF16)] * parts,
        compiler_params=pltpu.CompilerParams(vmem_limit_bytes=VMEM_LIMIT),
        cost_estimate=COST,
        name="turn",
    )(layer, w_out, x2, dx, core, near, dy, ot, gains)
    return *out[:3], out[3:]


def finish_kernel(parts, layer, *refs):
    part_refs, refs = refs[:parts], refs[parts:]
    w_ref, x_ref, dx2_ref, gain_ref, out_ref = refs
    width = w_ref.shape[2]
    grad = None
    for part in range(parts):
        for item in range(3):
            value = part_refs[part][item * width : (item + 1) * width, :]
            term = dot(value.T, w_ref[layer[0] ^ part, item])
            grad = term if grad is None else grad + term
    back, _ = norm_backward(x_ref[...].astype(F32), gain_ref[0:1, :].astype(F32), grad)
    out_ref[...] = (dx2_ref[...] + back).astype(BF16)


def finish(layer, parts, w_qkv, rows, dx2, gains):
    count, dim = rows.shape
    return pl.pallas_call(
        partial(finish_kernel, len(parts)),
        in_specs=[pl.BlockSpec(memory_space=pltpu.SMEM)] + [vmem()] * (len(parts) + 4),
        out_specs=vmem(),
        out_shape=jax.ShapeDtypeStruct((count, dim), BF16),
        compiler_params=pltpu.CompilerParams(vmem_limit_bytes=VMEM_LIMIT),
        cost_estimate=COST,
        name="finish",
    )(layer, *parts, w_qkv, rows, dx2, gains)


def small_kernel(flat_ref, x_ref, w_ref, gain_ref, shift_ref, gout_ref, sums_ref, out_ref):
    dim = x_ref.shape[1]
    unit, _ = normalized(x_ref[...].astype(F32))
    inner = dot(flat_ref[...], unit.astype(BF16))
    sums = jnp.sum(flat_ref[...].astype(F32), axis=1, keepdims=True)
    grad = inner * gain_ref[0:1, :].astype(F32) + sums * shift_ref[0:1, :].astype(F32)
    width = w_ref.shape[1]
    gain = jnp.zeros((1, dim), F32)
    shift = jnp.zeros((1, dim), F32)
    for item in range(3):
        rows = slice(item * width, (item + 1) * width)
        w = w_ref[item].astype(F32)
        gain = gain + jnp.sum(w * inner[rows, :], axis=0, keepdims=True)
        shift = shift + jnp.sum(w * sums[rows, :], axis=0, keepdims=True)
    side = 3 * width
    out_ref[:, :dim] = gout_ref[...]
    out_ref[:, dim : dim + side] = grad.T.astype(BF16)
    sums = jnp.concatenate([gain, sums_ref[0:1, :], shift, sums_ref[1:2, :]], axis=0)
    sums = jnp.concatenate([sums, jnp.zeros((out_ref.shape[1] - dim - side - 4, dim), F32)], axis=0)
    out_ref[:, dim + side :] = sums.T.astype(BF16)


def small(flat, rows, w_qkv, gains, shifts, grad_out, sums):
    side, dim = flat.shape[0], rows.shape[1]
    total = -(-(dim + side + 8) // 128) * 128
    return pl.pallas_call(
        small_kernel,
        in_specs=[vmem()] * 7,
        out_specs=vmem(),
        out_shape=jax.ShapeDtypeStruct((dim, total), BF16),
        compiler_params=pltpu.CompilerParams(vmem_limit_bytes=VMEM_LIMIT),
        cost_estimate=COST,
        name="small",
    )(flat, rows, w_qkv, gains, shifts, grad_out, sums)


def collect_kernel(layer, *refs):
    parts, out_ref = refs[:-1], refs[-1]
    size = parts[0].shape[0]
    for item, part in enumerate(parts):
        out_ref[pl.ds(pl.multiple_of((layer[0] ^ item) * size, 128), size), :] = part[...]


def collect(layer, parts):
    size, dim = parts[0].shape
    return pl.pallas_call(
        collect_kernel,
        in_specs=[pl.BlockSpec(memory_space=pltpu.SMEM)] + [vmem()] * len(parts),
        out_specs=vmem(),
        out_shape=jax.ShapeDtypeStruct((size * len(parts), dim), parts[0].dtype),
        compiler_params=pltpu.CompilerParams(vmem_limit_bytes=VMEM_LIMIT),
        cost_estimate=COST,
        name="collect",
    )(layer, *parts)


def keep_kernel(source_ref, out_ref):
    out_ref[...] = source_ref[...]


def keep(value):
    return pl.pallas_call(
        keep_kernel,
        in_specs=[vmem()],
        out_specs=vmem(),
        out_shape=jax.ShapeDtypeStruct(value.shape, value.dtype),
        compiler_params=pltpu.CompilerParams(vmem_limit_bytes=VMEM_LIMIT),
        cost_estimate=COST,
        name="keep",
    )(value)


WIDE = ("far", "near", "core")


def swap(value, axis):
    return lax.ppermute(value, axis, [(0, 1), (1, 0)])


def spread(parts):
    size = len(parts)
    return [parts[0]] + [
        lax.ppermute(parts[bit], "narrow", [(i, i ^ bit) for i in range(size)])
        for bit in range(1, size)
    ]


def exchange(value, axis):
    return lax.all_to_all(value, axis, 0, 0, tiled=True)


def after(value, *others):
    return lax.optimization_barrier((value,) + others)[0]


def add(*parts):
    return sum(part.astype(F32) for part in parts).astype(BF16)


def local(
    tokens, cotangent, seq_lens, norm_gains, norm_shifts, w_qkv, w_attn_out, w_ffn_in, w_ffn_down
):
    depth = lax.axis_size("narrow")
    across = lax.axis_size(WIDE)
    count, dim = tokens.shape
    mine = count // depth
    width = w_qkv.shape[2]
    cols = w_ffn_in.shape[1]
    heads = width // HD
    layer = lax.axis_index("narrow")
    layers = layer.astype(jnp.int32).reshape(1)

    pieces = lax.all_gather(
        jnp.concatenate([jnp.swapaxes(w_qkv, 1, 2), w_attn_out[None]], axis=0), WIDE, axis=0
    )
    weights = lax.all_gather(
        jnp.concatenate([w_ffn_in, w_ffn_down], axis=1), ("far", "narrow"), axis=0, tiled=True
    )
    group = max(1, dim // cols)
    shape = (-1, group, dim, 2, cols)
    if group > 1:
        weights = weights.reshape(shape).transpose(0, 2, 3, 1, 4).reshape(-1, 2 * group * cols)
    rows = lax.dynamic_slice_in_dim(tokens, layer * mine, mine, 0)
    dy = lax.dynamic_slice_in_dim(cotangent, layer * mine, mine, 0)
    dy_near = swap(dy, "near")
    dy_own = (dy, swap(dy, "core"))
    dy_far = (dy_near, swap(dy_near, "core"))

    q_rows, k_rows, q_cols, k_cols, v_cols, *tables, w_proj, w_out = project(
        seq_lens, tokens, norm_gains, norm_shifts, pieces, depth
    )
    w_out = exchange(w_out, "narrow")
    parts, out, lse = attend(0, heads, depth, layers, tables, k_rows, q_cols, v_cols)
    x2, xn2, ot = mix(layers, spread(parts), w_out, rows, norm_gains, norm_shifts)
    xn_near = swap(xn2, "near")
    xn_own = (xn2, swap(xn2, "core"))
    w_proj_all = lax.all_gather(w_proj, "narrow", axis=0)

    y_a, dx_a, y_core, dx_core, g_a, du_a = ffn(xn_own, dy_own, weights)
    xn_near = after(xn_near, y_a)
    xn_far = (xn_near, swap(xn_near, "core"))
    y_b, dx_b, y_far, dx_far, g_b, du_b = ffn(xn_far, dy_far, weights)
    dx_core = swap(dx_core, "core")
    dx_near = swap(add(dx_b, swap(dx_far, "core")), "near")
    pair = lax.axis_size("far") == 2
    base = lax.axis_index("far") if pair else jnp.zeros((), jnp.int32)
    base = base.astype(jnp.int32).reshape(1)
    grads = outer(base, xn_own + xn_far, dy_own + dy_far, (g_a, g_b), (du_a, du_b), group * cols)
    dx2, grad_out, norm_two, dout = turn(
        layers, w_out, after(x2, grads), dx_a, dx_core, dx_near, dy, ot, norm_gains
    )
    dout = spread(dout)
    y_core, y_far = (swap(part, "core") for part in (y_core, y_far))
    y_near = swap(add(y_b, y_far), "near")
    out_mine = x2 + y_a.astype(F32) + y_core.astype(F32) + y_near.astype(F32)
    out_mine = out_mine.astype(BF16)
    dout, out_mine = lax.optimization_barrier((dout, out_mine))
    layer_out = lax.all_gather(out_mine, "narrow", axis=0, tiled=True)
    back, flat_back = attend_back(
        0, heads, layers, tables, q_rows, k_rows, q_cols, k_cols, v_cols, out, lse, dout
    )
    if pair:
        back, far_grads = lax.optimization_barrier((back, swap(grads[1], "far")))
        total = add(after(grads[0], flat_back), far_grads)
    else:
        grads = grads.reshape(-1, dim, 2, group, cols).transpose(0, 3, 1, 2, 4)
        grads = grads.reshape(-1, dim, 2 * cols)
        total = lax.psum_scatter(grads, "far", scatter_dimension=0, tiled=False)
    total = lax.psum_scatter(total, "narrow", scatter_dimension=0, tiled=True).astype(F32)

    back = spread(back)
    rest = small(flat_back, tokens, w_proj, norm_gains, norm_shifts, grad_out, norm_two)
    in_mine = finish(layers, back, w_proj_all, rows, after(dx2, rest), norm_gains)
    input_grad = lax.all_gather(in_mine, "narrow", axis=0, tiled=True)

    side = 3 * width
    part = dim // across
    rest = exchange(after(rest, in_mine).reshape(across, part, -1), WIDE)
    rest = jnp.sum(rest.astype(F32), axis=0)
    layer_out = keep(after(layer_out, rest))
    gqkv = rest[:, dim : dim + side].reshape(part, 3, width).transpose(1, 0, 2)
    gout = rest[:, :dim].astype(BF16).reshape(part, depth, width).transpose(1, 0, 2)
    norms = rest[:, dim + side : dim + side + 4].astype(BF16)
    gout = jnp.concatenate([gout, jnp.broadcast_to(norms, (depth, part, 4))], axis=2)
    gout = jnp.sum(exchange(gout, "narrow").astype(F32), axis=0).T
    gout, norms = gout[:width], gout[width:]
    return (
        layer_out,
        input_grad,
        norms[:2],
        norms[2:],
        gqkv,
        gout,
        total[:, :cols],
        total[:, cols:],
    )


def solution(mesh):
    depth, across = mesh.shape["narrow"], mesh.shape["wide"]
    fine = jax.sharding.Mesh(
        mesh.devices.reshape(depth, across // 4, 2, 2), ("narrow", "far", "near", "core")
    )
    return jax.shard_map(
        local,
        mesh=fine,
        in_specs=(
            P(WIDE, None),
            P(WIDE, None),
            P(WIDE, None),
            P(),
            P(),
            P(None, WIDE, "narrow"),
            P("narrow", WIDE),
            P("narrow", WIDE),
            P("narrow", WIDE),
        ),
        out_specs=(
            P(WIDE, None),
            P(WIDE, None),
            P(None, WIDE),
            P(None, WIDE),
            P(None, WIDE, "narrow"),
            P("narrow", WIDE),
            P("narrow", WIDE),
            P("narrow", WIDE),
        ),
        check_vma=False,
    )
```

```python
from functools import partial

import jax
import jax.numpy as jnp
from jax import lax
from jax.experimental import pallas as pl
from jax.experimental.pallas import tpu as pltpu
from jax.sharding import PartitionSpec as P

HD = 32
EPS = 1e-05
LOG2E = 1.4426950408889634
SCALE = HD ** (-0.5)
BQ = 256
BK = 256
STEP = 256
STEPS = 3
BF16 = jnp.bfloat16
F32 = jnp.float32
VMEM_LIMIT = 56 * 1024 * 1024
COST = pl.CostEstimate(flops=1000000, bytes_accessed=100000, transcendentals=0)


def vmem(*shape):
    return pl.BlockSpec(shape, None) if shape else pl.BlockSpec(memory_space=pltpu.VMEM)


def dot(a, b):
    return jnp.dot(a, b, preferred_element_type=F32)


def dot_nt(a, b):
    return lax.dot_general(a, b, (((1,), (1,)), ((), ())), preferred_element_type=F32)


def normalized(rows):
    center = rows - jnp.mean(rows, axis=-1, keepdims=True)
    spread = jnp.mean(center * center, axis=-1, keepdims=True)
    inverse = lax.rsqrt(spread + EPS)
    return center * inverse, inverse


def norm_backward(rows, gain, grad):
    unit, inverse = normalized(rows)
    scaled = grad * gain
    inner = scaled - jnp.mean(scaled, axis=-1, keepdims=True)
    inner = inner - unit * jnp.mean(scaled * unit, axis=-1, keepdims=True)
    return inverse * inner, grad * unit


def project_kernel(
    lens, x_ref, gain_ref, shift_ref, w_ref,
    q_ref, k_ref, qt_ref, kt_ref, vt_ref, seg_ref, bounds_ref, full_ref, out_ref,
):
    across = w_ref.shape[0]
    kinds = full_ref.shape[0] + 1
    narrow = w_ref.shape[2] // kinds

    @pl.when(pl.program_id(0) == 0)
    def _():
        for part in range(across):
            spot = slice(part * narrow, (part + 1) * narrow)
            for item in range(kinds - 1):
                full_ref[item, :, spot] = w_ref[part, :, item * narrow : (item + 1) * narrow]
            last = w_ref[part, :, (kinds - 1) * narrow :]
            for copy in range(out_ref.shape[0]):
                out_ref[copy, :, spot] = last

    size = x_ref.shape[0]
    first = pl.program_id(0) * size
    tiles = size // BQ
    end = jnp.int32(0)
    low = [jnp.int32(0)] * tiles
    high = [jnp.int32(0) + pl.num_programs(0) * size] * tiles
    cols = first + lax.broadcasted_iota(jnp.int32, seg_ref.shape, 1)
    segment = jnp.zeros(seg_ref.shape, jnp.int32)
    for item in range(lens.shape[1]):
        end = end + lens[0, item]
        for tile in range(tiles):
            start = first + tile * BQ
            low[tile] = jnp.where(end <= start, end, low[tile])
            later = (end > start + (BQ - 1)) & (end < high[tile])
            high[tile] = jnp.where(later, end, high[tile])
        segment = segment + (cols >= end).astype(jnp.int32)
    seg_ref[...] = segment.astype(F32)
    for tile in range(tiles):
        lowest = lax.div(low[tile], jnp.int32(STEP))
        highest = lax.div(high[tile] + (STEP - 1), jnp.int32(STEP))
        steps = lax.div((highest - lowest) * STEP + (BK - 1), jnp.int32(BK))
        room = pl.num_programs(0) * (size // STEP) - steps * (BK // STEP)
        block = pl.program_id(0) * tiles + tile
        bounds_ref[block, 0] = jnp.minimum(lowest, room)
        bounds_ref[block, 1] = steps
    unit, _ = normalized(x_ref[...].astype(F32))
    xn = (unit * gain_ref[0:1, :].astype(F32) + shift_ref[0:1, :].astype(F32)).astype(BF16)
    for item, (rows_ref, cols_ref) in enumerate(((q_ref, qt_ref), (k_ref, kt_ref), (None, vt_ref))):
        cols_ref[...] = dot_nt(full_ref[item], xn).astype(BF16)
        if rows_ref is not None:
            full = dot_nt(xn, full_ref[item]).astype(BF16)
            for head in range(q_ref.shape[0]):
                rows_ref[head] = full[:, head * HD : (head + 1) * HD]


def project(lens, tokens, gains, shifts, weights, depth):
    count, dim = tokens.shape
    width = weights.shape[1]
    blocks = count // BQ
    size = count // STEPS
    heads = width // HD
    per_head = pl.BlockSpec((heads, size, HD), lambda i: (0, i, 0))
    turned = pl.BlockSpec((width, size), lambda i: (0, i))
    fixed2 = pl.BlockSpec((2, dim), lambda i: (0, 0))
    return pl.pallas_call(
        project_kernel,
        grid=(STEPS,),
        in_specs=[
            pl.BlockSpec(memory_space=pltpu.SMEM),
            pl.BlockSpec((size, dim), lambda i: (i, 0)),
            fixed2,
            fixed2,
            pl.BlockSpec(weights.shape, lambda i: (0, 0, 0)),
        ],
        out_specs=[
            per_head,
            per_head,
            turned,
            turned,
            turned,
            pl.BlockSpec((8, size), lambda i: (0, i)),
            pl.BlockSpec(memory_space=pltpu.SMEM),
            pl.BlockSpec((3, width, dim), lambda i: (0, 0, 0)),
            pl.BlockSpec((depth, width, dim), lambda i: (0, 0, 0)),
        ],
        out_shape=[
            jax.ShapeDtypeStruct((heads, count, HD), BF16),
            jax.ShapeDtypeStruct((heads, count, HD), BF16),
            jax.ShapeDtypeStruct((width, count), BF16),
            jax.ShapeDtypeStruct((width, count), BF16),
            jax.ShapeDtypeStruct((width, count), BF16),
            jax.ShapeDtypeStruct((8, count), F32),
            jax.ShapeDtypeStruct((blocks, 2), jnp.int32),
            jax.ShapeDtypeStruct((3, width, dim), BF16),
            jax.ShapeDtypeStruct((depth, width, dim), BF16),
        ],
        compiler_params=pltpu.CompilerParams(vmem_limit_bytes=VMEM_LIMIT),
        cost_estimate=COST,
        name="project",
    )(lens, tokens, gains, shifts, weights)


def spread_lanes(column, width):
    return jnp.concatenate([column] * (width // 128), axis=1) if width > 128 else column


def spot_of(layer, item, size):
    return pl.ds(pl.multiple_of((layer[0] ^ item) * size, 128), size)


def column_of(row_ref, column_ref):
    for start in range(0, column_ref.shape[0], BK):
        turned = row_ref[:, start : start + BK].T
        column_ref[start : start + BK, :] = jnp.broadcast_to(turned[:, 0:1], (BK, 128))


def attend_kernel(
    first, heads, parts, layer, bounds, segr_ref, k_ref, qt_ref, vt_ref, *refs
):
    part_refs, (ot_ref, lse_ref, segc_ref) = refs[:parts], refs[parts:]
    count = segc_ref.shape[0]
    column_of(segr_ref, segc_ref)
    factor = SCALE * LOG2E

    def q_block(block, _):
        start = pl.multiple_of(block * BQ, BQ)
        seg_q = segr_ref[0:1, pl.ds(start, BQ)]
        queries = [
            qt_ref[(first + h) * HD : (first + h + 1) * HD, pl.ds(start, BQ)] for h in range(heads)
        ]

        def k_block(item, carry):
            at = pl.multiple_of(bounds[block, 0] * STEP + item * BK, STEP)
            allowed = spread_lanes(segc_ref[pl.ds(at, BK), :], BQ) == seg_q
            out = []
            scores = [dot(k_ref[first + h, pl.ds(at, BK), :], queries[h]) for h in range(heads)]
            scores = [jnp.where(allowed, value, -1e30) for value in scores]
            fresh = [
                jnp.maximum(carry[h][0], jnp.max(scores[h], axis=0, keepdims=True))
                for h in range(heads)
            ]
            expd = [jnp.exp2((scores[h] - fresh[h]) * factor) for h in range(heads)]
            for h in range(heads):
                top, total, acc = carry[h]
                fade = jnp.exp2((top - fresh[h]) * factor)
                total = total * fade + jnp.sum(expd[h], axis=0, keepdims=True)
                rows = vt_ref[(first + h) * HD : (first + h + 1) * HD, pl.ds(at, BK)]
                acc = acc * fade + dot(rows, expd[h].astype(BF16))
                out.append((fresh[h], total, acc))
            return tuple(out)

        empty = (
            jnp.full((1, BQ), -1e30, F32),
            jnp.zeros((1, BQ), F32),
            jnp.zeros((HD, BQ), F32),
        )
        done = lax.fori_loop(0, bounds[block, 1], k_block, (empty,) * heads)
        for h in range(heads):
            top, total, acc = done[h]
            ot_ref[h * HD : (h + 1) * HD, pl.ds(start, BQ)] = (acc / total).astype(BF16)
            lse_ref[h : h + 1, pl.ds(start, BQ)] = top * factor + jnp.log(total) * LOG2E
        return 0

    lax.fori_loop(0, count // BQ, q_block, 0)
    size = count // parts
    for part in range(parts):
        part_refs[part][...] = ot_ref[:, spot_of(layer, part, size)]


def attend(first, heads, parts, layer, tables, k_rows, q_cols, v_cols):
    segr, bounds = tables
    count = segr.shape[1]
    out = pl.pallas_call(
        partial(attend_kernel, first, heads, parts),
        in_specs=[pl.BlockSpec(memory_space=pltpu.SMEM)] * 2 + [vmem()] * 4,
        out_specs=[vmem()] * (parts + 2),
        out_shape=[jax.ShapeDtypeStruct((heads * HD, count // parts), BF16)] * parts
        + [
            jax.ShapeDtypeStruct((heads * HD, count), BF16),
            jax.ShapeDtypeStruct((8, count), F32),
        ],
        scratch_shapes=[pltpu.VMEM((count, 128), F32)],
        compiler_params=pltpu.CompilerParams(vmem_limit_bytes=VMEM_LIMIT),
        cost_estimate=COST,
        name=f"attend_{first}",
    )(layer, bounds, segr, k_rows, q_cols, v_cols)
    return out[:parts], out[parts], out[parts + 1]


def attend_back_kernel(
    first, heads, parts, layer, bounds, segr_ref,
    q_ref, k_ref, qt_ref, kt_ref, vt_ref, ot_ref, lse_ref, *refs,
):
    part_refs, out_refs, refs = refs[:parts], refs[parts : 2 * parts], refs[2 * parts :]
    flat_ref, segc_ref, dot_ref, do_ref, stat_ref, dq_ref, dqt_ref, dkt_ref, dvt_ref = refs
    count = segc_ref.shape[0]
    column_of(segr_ref, segc_ref)
    factor = SCALE * LOG2E
    size = count // parts
    for part in range(parts):
        value = part_refs[part][first * HD : (first + heads) * HD, :]
        dot_ref[:, spot_of(layer, part, size)] = value
        for h in range(heads):
            do_ref[h, spot_of(layer, part, size), :] = value[h * HD : (h + 1) * HD, :].T
    dkt_ref[...] = jnp.zeros_like(dkt_ref)
    dvt_ref[...] = jnp.zeros_like(dvt_ref)

    def q_block(block, _):
        start = pl.multiple_of(block * BQ, BQ)
        spot = pl.ds(start, BQ)
        stats = [lse_ref[0:heads, spot]]
        for h in range(heads):
            lane = slice(h * HD, (h + 1) * HD)
            stats.append(
                jnp.sum(
                    dot_ref[lane, spot].astype(F32) * ot_ref[lane, spot].astype(F32),
                    axis=0,
                    keepdims=True,
                )
            )
        stats.append(jnp.zeros((8 - 2 * heads, BQ), F32)) if heads < 4 else None
        turned = jnp.concatenate(stats, axis=0).T
        for h in range(2 * heads):
            stat_ref[h] = jnp.broadcast_to(turned[:, h : h + 1], (BQ, 128))
        dq_ref[...] = jnp.zeros_like(dq_ref)
        seg_q = spread_lanes(segc_ref[spot, :], BK)

        def k_block(item, _):
            at = pl.multiple_of(bounds[block, 0] * STEP + item * BK, STEP)
            here = pl.ds(at, BK)
            allowed = seg_q == segr_ref[0:1, here]
            lanes = [slice(h * HD, (h + 1) * HD) for h in range(heads)]
            owns = [slice((first + h) * HD, (first + h + 1) * HD) for h in range(heads)]
            scores = [dot(q_ref[first + h, spot, :], kt_ref[owns[h], here]) for h in range(heads)]
            dprob = [dot(do_ref[h, spot, :], vt_ref[owns[h], here]) for h in range(heads)]
            prob = [
                jnp.where(
                    allowed, jnp.exp2(scores[h] * factor - spread_lanes(stat_ref[h], BK)), 0.0
                )
                for h in range(heads)
            ]
            dscore = [
                (prob[h] * (dprob[h] - spread_lanes(stat_ref[heads + h], BK))).astype(BF16)
                for h in range(heads)
            ]
            for h in range(heads):
                dvt_ref[lanes[h], here] += dot(dot_ref[lanes[h], spot], prob[h].astype(BF16))
                dkt_ref[lanes[h], here] += dot(qt_ref[owns[h], spot], dscore[h])
                dq_ref[h] += dot(dscore[h], k_ref[first + h, here, :])
            return 0

        lax.fori_loop(0, bounds[block, 1], k_block, 0)
        for h in range(heads):
            dqt_ref[h * HD : (h + 1) * HD, spot] = dq_ref[h].T * SCALE
        return 0

    lax.fori_loop(0, count // BQ, q_block, 0)
    width = heads * HD
    for item, (source, scale) in enumerate(((dqt_ref, 1.0), (dkt_ref, SCALE), (dvt_ref, 1.0))):
        value = source[...] if scale == 1.0 else source[...] * scale
        value = value.astype(BF16)
        flat_ref[item * width : (item + 1) * width, :] = value
    for part in range(parts):
        out_refs[part][...] = flat_ref[:, spot_of(layer, part, size)]


def attend_back(first, heads, layer, tables, q_rows, k_rows, q_cols, k_cols, v_cols, out, lse, dout):
    segr, bounds = tables
    count = segr.shape[1]
    parts = len(dout)
    width = heads * HD
    result = pl.pallas_call(
        partial(attend_back_kernel, first, heads, parts),
        in_specs=[pl.BlockSpec(memory_space=pltpu.SMEM)] * 2 + [vmem()] * (8 + parts),
        out_specs=[vmem()] * (parts + 1),
        out_shape=[jax.ShapeDtypeStruct((3 * width, count // parts), BF16)] * parts
        + [jax.ShapeDtypeStruct((3 * width, count), BF16)],
        scratch_shapes=[
            pltpu.VMEM((count, 128), F32),
            pltpu.VMEM((width, count), BF16),
            pltpu.VMEM((heads, count, HD), BF16),
            pltpu.VMEM((2 * heads, BQ, 128), F32),
            pltpu.VMEM((heads, BQ, HD), F32),
            pltpu.VMEM((width, count), F32),
            pltpu.VMEM((width, count), F32),
            pltpu.VMEM((width, count), F32),
        ],
        compiler_params=pltpu.CompilerParams(vmem_limit_bytes=VMEM_LIMIT),
        cost_estimate=COST,
        name=f"attend_back_{first}",
    )(layer, bounds, segr, q_rows, k_rows, q_cols, k_cols, v_cols, out, lse, *dout)
    return result[:parts], result[parts]


def mix_kernel(parts, layer, *refs):
    ot_refs, w_ref, refs = refs[:parts], refs[parts], refs[parts + 1 :]
    x_ref, gain_ref, shift_ref, x2_ref, xn_ref, ot_ref = refs
    middle = x_ref[...].astype(F32)
    for part in range(parts):
        value = ot_refs[part][...]
        ot_ref[layer[0] ^ part] = value
        middle = middle + dot(value.T, w_ref[layer[0] ^ part])
    x2_ref[...] = middle
    unit, _ = normalized(middle)
    xn_ref[...] = (unit * gain_ref[1:2, :].astype(F32) + shift_ref[1:2, :].astype(F32)).astype(BF16)


def mix(layer, ot, w_out, rows, gains, shifts):
    count, dim = rows.shape
    parts = len(ot)
    return pl.pallas_call(
        partial(mix_kernel, parts),
        in_specs=[pl.BlockSpec(memory_space=pltpu.SMEM)] + [vmem()] * (parts + 4),
        out_specs=[vmem()] * 3,
        out_shape=[
            jax.ShapeDtypeStruct((count, dim), F32),
            jax.ShapeDtypeStruct((count, dim), BF16),
            jax.ShapeDtypeStruct((parts,) + ot[0].shape, BF16),
        ],
        compiler_params=pltpu.CompilerParams(vmem_limit_bytes=VMEM_LIMIT),
        cost_estimate=COST,
        name="mix",
    )(layer, *ot, w_out, rows, gains, shifts)


def ffn_kernel(*refs):
    xn_parts, dy_parts, w_ref = refs[:2], refs[2:4], refs[4]
    outs, (g_ref, du_ref) = refs[5:9], refs[9:11]
    y_ref, dx_ref, xn_ref, dy_ref = refs[11:]
    item, side = pl.program_id(0), pl.program_id(1)
    mine, hidden = g_ref.shape
    spot = pl.ds(pl.multiple_of(side * mine, mine), mine)

    @pl.when((item == 0) & (side == 0))
    def _():
        for part in range(2):
            xn_ref[part * mine : (part + 1) * mine, :] = xn_parts[part][...]
            dy_ref[part * mine : (part + 1) * mine, :] = dy_parts[part][...]
        y_ref[...] = jnp.zeros_like(y_ref)
        dx_ref[...] = jnp.zeros_like(dx_ref)

    w_in = w_ref.at[:, :hidden]
    w_down = w_ref.at[:, hidden:]
    u = dot(xn_ref[spot, :], w_in[...])
    dg = dot(dy_ref[spot, :], w_down[...])
    half = 0.5 + 0.5 * lax.erf(u * 0.7071067811865476)
    slope = half + u * (jnp.exp2(u * u * (-0.5 * LOG2E)) * 0.3989422804014327)
    g = (u * half).astype(BF16)
    du = (dg * slope).astype(BF16)
    g_ref[...] = g
    du_ref[...] = du
    y_ref[spot, :] += dot_nt(g, w_down[...])
    dx_ref[spot, :] += dot_nt(du, w_in[...])

    @pl.when((item == pl.num_programs(0) - 1) & (side == 1))
    def _():
        outs[0][...] = y_ref[:mine, :].astype(BF16)
        outs[1][...] = dx_ref[:mine, :].astype(BF16)
        outs[2][...] = y_ref[mine:, :].astype(BF16)
        outs[3][...] = dx_ref[mine:, :].astype(BF16)


def ffn(xn, dy, weights):
    mine, dim = xn[0].shape
    count = 2 * mine
    blocks = weights.shape[0] // dim
    hidden = weights.shape[1] // 2
    whole = pl.BlockSpec((mine, dim), lambda i, j: (0, 0))
    act = pl.BlockSpec((mine, hidden), lambda i, j: (j, i))
    return pl.pallas_call(
        ffn_kernel,
        grid=(blocks, 2),
        in_specs=[whole] * 4 + [pl.BlockSpec((dim, 2 * hidden), lambda i, j: (i, 0))],
        out_specs=[whole] * 4 + [act] * 2,
        out_shape=[jax.ShapeDtypeStruct((mine, dim), BF16)] * 4
        + [jax.ShapeDtypeStruct((count, blocks * hidden), BF16)] * 2,
        scratch_shapes=[pltpu.VMEM((count, dim), F32)] * 2 + [pltpu.VMEM((count, dim), BF16)] * 2,
        compiler_params=pltpu.CompilerParams(vmem_limit_bytes=VMEM_LIMIT),
        cost_estimate=COST,
        name="ffn",
    )(*xn, *dy, weights)


def outer_kernel(sides, _, *refs):
    xn_parts, dy_parts = refs[: 2 * sides], refs[2 * sides : 4 * sides]
    g_refs, du_refs = refs[4 * sides : 5 * sides], refs[5 * sides : 6 * sides]
    grad_ref, xnt_ref, dyt_ref = refs[6 * sides :]
    mine = xn_parts[0].shape[0]
    hidden = g_refs[0].shape[1]

    @pl.when(pl.program_id(0) == 0)
    def _():
        for part in range(2 * sides):
            xnt_ref[:, part * mine : (part + 1) * mine] = xn_parts[part][...].T
            dyt_ref[:, part * mine : (part + 1) * mine] = dy_parts[part][...].T

    for at, turned, sources in ((0, xnt_ref, du_refs), (hidden, dyt_ref, g_refs)):
        total = None
        for side in range(sides):
            cut = slice(2 * side * mine, 2 * (side + 1) * mine)
            term = dot(turned[:, cut], sources[side][...])
            total = term if total is None else total + term
        grad_ref[0, :, at : at + hidden] = total.astype(BF16)


def outer(base, xn, dy, g, du, hidden):
    sides = len(g)
    mine, dim = xn[0].shape
    count = 2 * mine
    blocks = g[0].shape[1] // hidden
    whole = pl.BlockSpec((mine, dim), lambda i, base: (0, 0))
    act = pl.BlockSpec((count, hidden), lambda i, base: (0, i ^ base[0]))
    return pl.pallas_call(
        partial(outer_kernel, sides),
        grid_spec=pltpu.PrefetchScalarGridSpec(
            num_scalar_prefetch=1,
            grid=(blocks,),
            in_specs=[whole] * (4 * sides) + [act] * (2 * sides),
            out_specs=pl.BlockSpec((1, dim, 2 * hidden), lambda i, base: (i, 0, 0)),
            scratch_shapes=[pltpu.VMEM((dim, sides * count), BF16)] * 2,
        ),
        out_shape=jax.ShapeDtypeStruct((blocks, dim, 2 * hidden), BF16),
        compiler_params=pltpu.CompilerParams(vmem_limit_bytes=VMEM_LIMIT),
        cost_estimate=COST,
        name="outer",
    )(base, *xn, *dy, *g, *du)


def turn_kernel(layer, w_ref, *refs):
    x2_ref, dx_ref, core_ref, near_ref, dy_ref, ot_ref, gain_ref = refs[:7]
    dx2_ref, gout_ref, sums_ref = refs[7:10]
    dot_refs = refs[10:]
    middle = x2_ref[...]
    grad = dx_ref[...].astype(F32) + core_ref[...].astype(F32) + near_ref[...].astype(F32)
    back, prod = norm_backward(middle, gain_ref[1:2, :].astype(F32), grad)
    dx2 = dy_ref[...].astype(F32) + back
    dx2_ref[...] = dx2
    sums_ref[...] = jnp.concatenate(
        [
            jnp.sum(prod, axis=0, keepdims=True),
            jnp.sum(grad, axis=0, keepdims=True),
            jnp.zeros((6, grad.shape[1]), F32),
        ],
        axis=0,
    )
    low = dx2.astype(BF16)
    across = low.T
    width = ot_ref.shape[1]
    for part in range(w_ref.shape[0]):
        dot_refs[part][...] = dot(w_ref[layer[0] ^ part], across).astype(BF16)
        gout_ref[:, part * width : (part + 1) * width] = dot_nt(across, ot_ref[part]).astype(BF16)


def turn(layer, w_out, x2, dx, core, near, dy, ot, gains):
    count, dim = x2.shape
    parts = w_out.shape[0]
    out = pl.pallas_call(
        turn_kernel,
        in_specs=[pl.BlockSpec(memory_space=pltpu.SMEM)] + [vmem()] * 8,
        out_specs=[vmem()] * (parts + 3),
        out_shape=[
            jax.ShapeDtypeStruct((count, dim), F32),
            jax.ShapeDtypeStruct((dim, dim), BF16),
            jax.ShapeDtypeStruct((8, dim), F32),
        ]
        + [jax.ShapeDtypeStruct(ot.shape[1:], BF16)] * parts,
        compiler_params=pltpu.CompilerParams(vmem_limit_bytes=VMEM_LIMIT),
        cost_estimate=COST,
        name="turn",
    )(layer, w_out, x2, dx, core, near, dy, ot, gains)
    return *out[:3], out[3:]


def finish_kernel(parts, layer, *refs):
    part_refs, refs = refs[:parts], refs[parts:]
    w_ref, x_ref, dx2_ref, gain_ref, out_ref = refs
    width = w_ref.shape[2]
    grad = None
    for part in range(parts):
        for item in range(3):
            value = part_refs[part][item * width : (item + 1) * width, :]
            term = dot(value.T, w_ref[layer[0] ^ part, item])
            grad = term if grad is None else grad + term
    back, _ = norm_backward(x_ref[...].astype(F32), gain_ref[0:1, :].astype(F32), grad)
    out_ref[...] = (dx2_ref[...] + back).astype(BF16)


def finish(layer, parts, w_qkv, rows, dx2, gains):
    count, dim = rows.shape
    return pl.pallas_call(
        partial(finish_kernel, len(parts)),
        in_specs=[pl.BlockSpec(memory_space=pltpu.SMEM)] + [vmem()] * (len(parts) + 4),
        out_specs=vmem(),
        out_shape=jax.ShapeDtypeStruct((count, dim), BF16),
        compiler_params=pltpu.CompilerParams(vmem_limit_bytes=VMEM_LIMIT),
        cost_estimate=COST,
        name="finish",
    )(layer, *parts, w_qkv, rows, dx2, gains)


def small_kernel(flat_ref, x_ref, w_ref, gain_ref, shift_ref, gout_ref, sums_ref, out_ref):
    dim = x_ref.shape[1]
    unit, _ = normalized(x_ref[...].astype(F32))
    inner = dot(flat_ref[...], unit.astype(BF16))
    sums = jnp.sum(flat_ref[...].astype(F32), axis=1, keepdims=True)
    grad = inner * gain_ref[0:1, :].astype(F32) + sums * shift_ref[0:1, :].astype(F32)
    width = w_ref.shape[1]
    gain = jnp.zeros((1, dim), F32)
    shift = jnp.zeros((1, dim), F32)
    for item in range(3):
        rows = slice(item * width, (item + 1) * width)
        w = w_ref[item].astype(F32)
        gain = gain + jnp.sum(w * inner[rows, :], axis=0, keepdims=True)
        shift = shift + jnp.sum(w * sums[rows, :], axis=0, keepdims=True)
    side = 3 * width
    out_ref[:, :dim] = gout_ref[...]
    out_ref[:, dim : dim + side] = grad.T.astype(BF16)
    sums = jnp.concatenate([gain, sums_ref[0:1, :], shift, sums_ref[1:2, :]], axis=0)
    sums = jnp.concatenate([sums, jnp.zeros((out_ref.shape[1] - dim - side - 4, dim), F32)], axis=0)
    out_ref[:, dim + side :] = sums.T.astype(BF16)


def small(flat, rows, w_qkv, gains, shifts, grad_out, sums):
    side, dim = flat.shape[0], rows.shape[1]
    total = -(-(dim + side + 8) // 128) * 128
    return pl.pallas_call(
        small_kernel,
        in_specs=[vmem()] * 7,
        out_specs=vmem(),
        out_shape=jax.ShapeDtypeStruct((dim, total), BF16),
        compiler_params=pltpu.CompilerParams(vmem_limit_bytes=VMEM_LIMIT),
        cost_estimate=COST,
        name="small",
    )(flat, rows, w_qkv, gains, shifts, grad_out, sums)


def collect_kernel(layer, *refs):
    parts, out_ref = refs[:-1], refs[-1]
    size = parts[0].shape[0]
    for item, part in enumerate(parts):
        out_ref[pl.ds(pl.multiple_of((layer[0] ^ item) * size, 128), size), :] = part[...]


def collect(layer, parts):
    size, dim = parts[0].shape
    return pl.pallas_call(
        collect_kernel,
        in_specs=[pl.BlockSpec(memory_space=pltpu.SMEM)] + [vmem()] * len(parts),
        out_specs=vmem(),
        out_shape=jax.ShapeDtypeStruct((size * len(parts), dim), parts[0].dtype),
        compiler_params=pltpu.CompilerParams(vmem_limit_bytes=VMEM_LIMIT),
        cost_estimate=COST,
        name="collect",
    )(layer, *parts)


def keep_kernel(source_ref, out_ref):
    out_ref[...] = source_ref[...]


def keep(value):
    return pl.pallas_call(
        keep_kernel,
        in_specs=[vmem()],
        out_specs=vmem(),
        out_shape=jax.ShapeDtypeStruct(value.shape, value.dtype),
        compiler_params=pltpu.CompilerParams(vmem_limit_bytes=VMEM_LIMIT),
        cost_estimate=COST,
        name="keep",
    )(value)


WIDE = ("far", "near", "core")


def swap(value, axis):
    return lax.ppermute(value, axis, [(0, 1), (1, 0)])


def spread(parts):
    size = len(parts)
    return [parts[0]] + [
        lax.ppermute(parts[bit], "narrow", [(i, i ^ bit) for i in range(size)])
        for bit in range(1, size)
    ]


def exchange(value, axis):
    return lax.all_to_all(value, axis, 0, 0, tiled=True)


def after(value, *others):
    return lax.optimization_barrier((value,) + others)[0]


def add(*parts):
    return sum(part.astype(F32) for part in parts).astype(BF16)


def local(
    tokens, cotangent, seq_lens, norm_gains, norm_shifts, w_qkv, w_attn_out, w_ffn_in, w_ffn_down
):
    depth = lax.axis_size("narrow")
    across = lax.axis_size(WIDE)
    count, dim = tokens.shape
    mine = count // depth
    width = w_qkv.shape[2]
    cols = w_ffn_in.shape[1]
    heads = width // HD
    layer = lax.axis_index("narrow")
    layers = layer.astype(jnp.int32).reshape(1)

    pieces = lax.all_gather(
        jnp.concatenate([w_qkv.transpose(2, 0, 1).reshape(width, -1), w_attn_out], axis=1),
        WIDE,
        axis=0,
    )
    weights = lax.all_gather(
        jnp.concatenate([w_ffn_in, w_ffn_down], axis=1), ("far", "narrow"), axis=0, tiled=True
    )
    group = max(1, dim // cols)
    shape = (-1, group, dim, 2, cols)
    if group > 1:
        weights = weights.reshape(shape).transpose(0, 2, 3, 1, 4).reshape(-1, 2 * group * cols)
    rows = lax.dynamic_slice_in_dim(tokens, layer * mine, mine, 0)
    dy = lax.dynamic_slice_in_dim(cotangent, layer * mine, mine, 0)
    dy_near = swap(dy, "near")
    dy_own = (dy, swap(dy, "core"))
    dy_far = (dy_near, swap(dy_near, "core"))

    q_rows, k_rows, q_cols, k_cols, v_cols, *tables, w_proj, w_out = project(
        seq_lens, tokens, norm_gains, norm_shifts, pieces, depth
    )
    w_out = exchange(w_out, "narrow")
    parts, out, lse = attend(0, heads, depth, layers, tables, k_rows, q_cols, v_cols)
    x2, xn2, ot = mix(layers, spread(parts), w_out, rows, norm_gains, norm_shifts)
    xn_near = swap(xn2, "near")
    xn_own = (xn2, swap(xn2, "core"))
    w_proj_all = lax.all_gather(w_proj, "narrow", axis=0)

    y_a, dx_a, y_core, dx_core, g_a, du_a = ffn(xn_own, dy_own, weights)
    xn_near = after(xn_near, y_a)
    xn_far = (xn_near, swap(xn_near, "core"))
    y_b, dx_b, y_far, dx_far, g_b, du_b = ffn(xn_far, dy_far, weights)
    dx_core = swap(dx_core, "core")
    dx_near = swap(add(dx_b, swap(dx_far, "core")), "near")
    pair = lax.axis_size("far") == 2
    base = lax.axis_index("far") if pair else jnp.zeros((), jnp.int32)
    base = base.astype(jnp.int32).reshape(1)
    grads = outer(base, xn_own + xn_far, dy_own + dy_far, (g_a, g_b), (du_a, du_b), group * cols)
    dx2, grad_out, norm_two, dout = turn(
        layers, w_out, after(x2, grads), dx_a, dx_core, dx_near, dy, ot, norm_gains
    )
    dout = spread(dout)
    y_core, y_far = (swap(part, "core") for part in (y_core, y_far))
    y_near = swap(add(y_b, y_far), "near")
    out_mine = x2 + y_a.astype(F32) + y_core.astype(F32) + y_near.astype(F32)
    out_mine = out_mine.astype(BF16)
    dout, out_mine = lax.optimization_barrier((dout, out_mine))
    layer_out = lax.all_gather(out_mine, "narrow", axis=0, tiled=True)
    back, flat_back = attend_back(
        0, heads, layers, tables, q_rows, k_rows, q_cols, k_cols, v_cols, out, lse, dout
    )
    if pair:
        back, far_grads = lax.optimization_barrier((back, swap(grads[1], "far")))
        total = add(after(grads[0], flat_back), far_grads)
    else:
        grads = grads.reshape(-1, dim, 2, group, cols).transpose(0, 3, 1, 2, 4)
        grads = grads.reshape(-1, dim, 2 * cols)
        total = lax.psum_scatter(grads, "far", scatter_dimension=0, tiled=False)
    total = lax.psum_scatter(total, "narrow", scatter_dimension=0, tiled=True).astype(F32)

    back = spread(back)
    rest = small(flat_back, tokens, w_proj, norm_gains, norm_shifts, grad_out, norm_two)
    in_mine = finish(layers, back, w_proj_all, rows, after(dx2, rest), norm_gains)
    input_grad = lax.all_gather(in_mine, "narrow", axis=0, tiled=True)

    side = 3 * width
    part = dim // across
    rest = exchange(after(rest, in_mine).reshape(across, part, -1), WIDE)
    rest = jnp.sum(rest.astype(F32), axis=0)
    layer_out = keep(after(layer_out, rest))
    gqkv = rest[:, dim : dim + side].reshape(part, 3, width).transpose(1, 0, 2)
    gout = rest[:, :dim].astype(BF16).reshape(part, depth, width).transpose(1, 0, 2)
    norms = rest[:, dim + side : dim + side + 4].astype(BF16)
    gout = jnp.concatenate([gout, jnp.broadcast_to(norms, (depth, part, 4))], axis=2)
    gout = jnp.sum(exchange(gout, "narrow").astype(F32), axis=0).T
    gout, norms = gout[:width], gout[width:]
    return (
        layer_out,
        input_grad,
        norms[:2],
        norms[2:],
        gqkv,
        gout,
        total[:, :cols],
        total[:, cols:],
    )


def solution(mesh):
    depth, across = mesh.shape["narrow"], mesh.shape["wide"]
    fine = jax.sharding.Mesh(
        mesh.devices.reshape(depth, across // 4, 2, 2), ("narrow", "far", "near", "core")
    )
    return jax.shard_map(
        local,
        mesh=fine,
        in_specs=(
            P(WIDE, None),
            P(WIDE, None),
            P(WIDE, None),
            P(),
            P(),
            P(None, WIDE, "narrow"),
            P("narrow", WIDE),
            P("narrow", WIDE),
            P("narrow", WIDE),
        ),
        out_specs=(
            P(WIDE, None),
            P(WIDE, None),
            P(None, WIDE),
            P(None, WIDE),
            P(None, WIDE, "narrow"),
            P("narrow", WIDE),
            P("narrow", WIDE),
            P("narrow", WIDE),
        ),
        check_vma=False,
    )
```

```python
from functools import partial

import jax
import jax.numpy as jnp
from jax import lax
from jax.experimental import pallas as pl
from jax.experimental.pallas import tpu as pltpu
from jax.sharding import PartitionSpec as P

HD = 32
EPS = 1e-05
LOG2E = 1.4426950408889634
SCALE = HD ** (-0.5)
BQ = 256
BK = 256
STEP = 256
STEPS = 3
BF16 = jnp.bfloat16
F32 = jnp.float32
VMEM_LIMIT = 56 * 1024 * 1024
COST = pl.CostEstimate(flops=1000000, bytes_accessed=100000, transcendentals=0)


def vmem(*shape):
    return pl.BlockSpec(shape, None) if shape else pl.BlockSpec(memory_space=pltpu.VMEM)


def dot(a, b):
    return jnp.dot(a, b, preferred_element_type=F32)


def dot_nt(a, b):
    return lax.dot_general(a, b, (((1,), (1,)), ((), ())), preferred_element_type=F32)


def normalized(rows):
    center = rows - jnp.mean(rows, axis=-1, keepdims=True)
    spread = jnp.mean(center * center, axis=-1, keepdims=True)
    inverse = lax.rsqrt(spread + EPS)
    return center * inverse, inverse


def norm_backward(rows, gain, grad):
    unit, inverse = normalized(rows)
    scaled = grad * gain
    inner = scaled - jnp.mean(scaled, axis=-1, keepdims=True)
    inner = inner - unit * jnp.mean(scaled * unit, axis=-1, keepdims=True)
    return inverse * inner, grad * unit


def project_kernel(
    lens, x_ref, gain_ref, shift_ref, w_ref,
    q_ref, k_ref, qt_ref, kt_ref, vt_ref, seg_ref, bounds_ref, full_ref, out_ref,
):
    across = w_ref.shape[0]
    kinds = full_ref.shape[0] + 1
    narrow = w_ref.shape[2] // kinds

    @pl.when(pl.program_id(0) == 0)
    def _():
        for part in range(across):
            spot = slice(part * narrow, (part + 1) * narrow)
            for item in range(kinds - 1):
                full_ref[item, :, spot] = w_ref[part, :, item * narrow : (item + 1) * narrow]
            last = w_ref[part, :, (kinds - 1) * narrow :]
            for copy in range(out_ref.shape[0]):
                out_ref[copy, :, spot] = last

    size = x_ref.shape[0]
    first = pl.program_id(0) * size
    tiles = size // BQ
    end = jnp.int32(0)
    low = [jnp.int32(0)] * tiles
    high = [jnp.int32(0) + pl.num_programs(0) * size] * tiles
    cols = first + lax.broadcasted_iota(jnp.int32, seg_ref.shape, 1)
    segment = jnp.zeros(seg_ref.shape, jnp.int32)
    for item in range(lens.shape[1]):
        end = end + lens[0, item]
        for tile in range(tiles):
            start = first + tile * BQ
            low[tile] = jnp.where(end <= start, end, low[tile])
            later = (end > start + (BQ - 1)) & (end < high[tile])
            high[tile] = jnp.where(later, end, high[tile])
        segment = segment + (cols >= end).astype(jnp.int32)
    seg_ref[...] = segment.astype(F32)
    for tile in range(tiles):
        lowest = lax.div(low[tile], jnp.int32(STEP))
        highest = lax.div(high[tile] + (STEP - 1), jnp.int32(STEP))
        steps = lax.div((highest - lowest) * STEP + (BK - 1), jnp.int32(BK))
        room = pl.num_programs(0) * (size // STEP) - steps * (BK // STEP)
        block = pl.program_id(0) * tiles + tile
        bounds_ref[block, 0] = jnp.minimum(lowest, room)
        bounds_ref[block, 1] = steps
    unit, _ = normalized(x_ref[...].astype(F32))
    xn = (unit * gain_ref[0:1, :].astype(F32) + shift_ref[0:1, :].astype(F32)).astype(BF16)
    for item, (rows_ref, cols_ref) in enumerate(((q_ref, qt_ref), (k_ref, kt_ref), (None, vt_ref))):
        cols_ref[...] = dot_nt(full_ref[item], xn).astype(BF16)
        if rows_ref is not None:
            full = dot_nt(xn, full_ref[item]).astype(BF16)
            for head in range(q_ref.shape[0]):
                rows_ref[head] = full[:, head * HD : (head + 1) * HD]


def project(lens, tokens, gains, shifts, weights, depth):
    count, dim = tokens.shape
    width = weights.shape[1]
    blocks = count // BQ
    size = count // STEPS
    heads = width // HD
    per_head = pl.BlockSpec((heads, size, HD), lambda i: (0, i, 0))
    turned = pl.BlockSpec((width, size), lambda i: (0, i))
    fixed2 = pl.BlockSpec((2, dim), lambda i: (0, 0))
    return pl.pallas_call(
        project_kernel,
        grid=(STEPS,),
        in_specs=[
            pl.BlockSpec(memory_space=pltpu.SMEM),
            pl.BlockSpec((size, dim), lambda i: (i, 0)),
            fixed2,
            fixed2,
            pl.BlockSpec(weights.shape, lambda i: (0, 0, 0)),
        ],
        out_specs=[
            per_head,
            per_head,
            turned,
            turned,
            turned,
            pl.BlockSpec((8, size), lambda i: (0, i)),
            pl.BlockSpec(memory_space=pltpu.SMEM),
            pl.BlockSpec((3, width, dim), lambda i: (0, 0, 0)),
            pl.BlockSpec((depth, width, dim), lambda i: (0, 0, 0)),
        ],
        out_shape=[
            jax.ShapeDtypeStruct((heads, count, HD), BF16),
            jax.ShapeDtypeStruct((heads, count, HD), BF16),
            jax.ShapeDtypeStruct((width, count), BF16),
            jax.ShapeDtypeStruct((width, count), BF16),
            jax.ShapeDtypeStruct((width, count), BF16),
            jax.ShapeDtypeStruct((8, count), F32),
            jax.ShapeDtypeStruct((blocks, 2), jnp.int32),
            jax.ShapeDtypeStruct((3, width, dim), BF16),
            jax.ShapeDtypeStruct((depth, width, dim), BF16),
        ],
        compiler_params=pltpu.CompilerParams(vmem_limit_bytes=VMEM_LIMIT),
        cost_estimate=COST,
        name="project",
    )(lens, tokens, gains, shifts, weights)


def spread_lanes(column, width):
    return jnp.concatenate([column] * (width // 128), axis=1) if width > 128 else column


def spot_of(layer, item, size):
    return pl.ds(pl.multiple_of((layer[0] ^ item) * size, 128), size)


def column_of(row_ref, column_ref):
    for start in range(0, column_ref.shape[0], BK):
        turned = row_ref[:, start : start + BK].T
        column_ref[start : start + BK, :] = jnp.broadcast_to(turned[:, 0:1], (BK, 128))


def attend_kernel(
    first, heads, parts, layer, bounds, segr_ref, k_ref, qt_ref, vt_ref, *refs
):
    part_refs, (ot_ref, lse_ref, segc_ref) = refs[:parts], refs[parts:]
    count = segc_ref.shape[0]
    column_of(segr_ref, segc_ref)
    factor = SCALE * LOG2E

    def q_block(block, _):
        start = pl.multiple_of(block * BQ, BQ)
        seg_q = segr_ref[0:1, pl.ds(start, BQ)]
        queries = [
            qt_ref[(first + h) * HD : (first + h + 1) * HD, pl.ds(start, BQ)] for h in range(heads)
        ]

        def k_block(item, carry):
            at = pl.multiple_of(bounds[block, 0] * STEP + item * BK, STEP)
            allowed = spread_lanes(segc_ref[pl.ds(at, BK), :], BQ) == seg_q
            out = []
            scores = [dot(k_ref[first + h, pl.ds(at, BK), :], queries[h]) for h in range(heads)]
            scores = [jnp.where(allowed, value, -1e30) for value in scores]
            fresh = [
                jnp.maximum(carry[h][0], jnp.max(scores[h], axis=0, keepdims=True))
                for h in range(heads)
            ]
            expd = [jnp.exp2((scores[h] - fresh[h]) * factor) for h in range(heads)]
            for h in range(heads):
                top, total, acc = carry[h]
                fade = jnp.exp2((top - fresh[h]) * factor)
                total = total * fade + jnp.sum(expd[h], axis=0, keepdims=True)
                rows = vt_ref[(first + h) * HD : (first + h + 1) * HD, pl.ds(at, BK)]
                acc = acc * fade + dot(rows, expd[h].astype(BF16))
                out.append((fresh[h], total, acc))
            return tuple(out)

        empty = (
            jnp.full((1, BQ), -1e30, F32),
            jnp.zeros((1, BQ), F32),
            jnp.zeros((HD, BQ), F32),
        )
        done = lax.fori_loop(0, bounds[block, 1], k_block, (empty,) * heads)
        for h in range(heads):
            top, total, acc = done[h]
            ot_ref[h * HD : (h + 1) * HD, pl.ds(start, BQ)] = (acc / total).astype(BF16)
            lse_ref[h : h + 1, pl.ds(start, BQ)] = top * factor + jnp.log(total) * LOG2E
        return 0

    lax.fori_loop(0, count // BQ, q_block, 0)
    size = count // parts
    for part in range(parts):
        part_refs[part][...] = ot_ref[:, spot_of(layer, part, size)]


def attend(first, heads, parts, layer, tables, k_rows, q_cols, v_cols):
    segr, bounds = tables
    count = segr.shape[1]
    out = pl.pallas_call(
        partial(attend_kernel, first, heads, parts),
        in_specs=[pl.BlockSpec(memory_space=pltpu.SMEM)] * 2 + [vmem()] * 4,
        out_specs=[vmem()] * (parts + 2),
        out_shape=[jax.ShapeDtypeStruct((heads * HD, count // parts), BF16)] * parts
        + [
            jax.ShapeDtypeStruct((heads * HD, count), BF16),
            jax.ShapeDtypeStruct((8, count), F32),
        ],
        scratch_shapes=[pltpu.VMEM((count, 128), F32)],
        compiler_params=pltpu.CompilerParams(vmem_limit_bytes=VMEM_LIMIT),
        cost_estimate=COST,
        name=f"attend_{first}",
    )(layer, bounds, segr, k_rows, q_cols, v_cols)
    return out[:parts], out[parts], out[parts + 1]


def attend_back_kernel(
    first, heads, parts, layer, bounds, segr_ref,
    q_ref, k_ref, qt_ref, kt_ref, vt_ref, ot_ref, lse_ref, *refs,
):
    part_refs, out_refs, refs = refs[:parts], refs[parts : 2 * parts], refs[2 * parts :]
    flat_ref, segc_ref, dot_ref, do_ref, stat_ref, dq_ref, dqt_ref, dkt_ref, dvt_ref = refs
    count = segc_ref.shape[0]
    column_of(segr_ref, segc_ref)
    factor = SCALE * LOG2E
    size = count // parts
    for part in range(parts):
        value = part_refs[part][first * HD : (first + heads) * HD, :]
        dot_ref[:, spot_of(layer, part, size)] = value
        for h in range(heads):
            do_ref[h, spot_of(layer, part, size), :] = value[h * HD : (h + 1) * HD, :].T
    dkt_ref[...] = jnp.zeros_like(dkt_ref)
    dvt_ref[...] = jnp.zeros_like(dvt_ref)

    def q_block(block, _):
        start = pl.multiple_of(block * BQ, BQ)
        spot = pl.ds(start, BQ)
        stats = [lse_ref[0:heads, spot]]
        for h in range(heads):
            lane = slice(h * HD, (h + 1) * HD)
            stats.append(
                jnp.sum(
                    dot_ref[lane, spot].astype(F32) * ot_ref[lane, spot].astype(F32),
                    axis=0,
                    keepdims=True,
                )
            )
        stats.append(jnp.zeros((8 - 2 * heads, BQ), F32)) if heads < 4 else None
        turned = jnp.concatenate(stats, axis=0).T
        for h in range(2 * heads):
            stat_ref[h] = jnp.broadcast_to(turned[:, h : h + 1], (BQ, 128))
        dq_ref[...] = jnp.zeros_like(dq_ref)
        seg_q = spread_lanes(segc_ref[spot, :], BK)

        def k_block(item, _):
            at = pl.multiple_of(bounds[block, 0] * STEP + item * BK, STEP)
            here = pl.ds(at, BK)
            allowed = seg_q == segr_ref[0:1, here]
            lanes = [slice(h * HD, (h + 1) * HD) for h in range(heads)]
            owns = [slice((first + h) * HD, (first + h + 1) * HD) for h in range(heads)]
            scores = [dot(q_ref[first + h, spot, :], kt_ref[owns[h], here]) for h in range(heads)]
            dprob = [dot(do_ref[h, spot, :], vt_ref[owns[h], here]) for h in range(heads)]
            prob = [
                jnp.where(
                    allowed, jnp.exp2(scores[h] * factor - spread_lanes(stat_ref[h], BK)), 0.0
                )
                for h in range(heads)
            ]
            dscore = [
                (prob[h] * (dprob[h] - spread_lanes(stat_ref[heads + h], BK))).astype(BF16)
                for h in range(heads)
            ]
            for h in range(heads):
                dvt_ref[lanes[h], here] += dot(dot_ref[lanes[h], spot], prob[h].astype(BF16))
                dkt_ref[lanes[h], here] += dot(qt_ref[owns[h], spot], dscore[h])
                dq_ref[h] += dot(dscore[h], k_ref[first + h, here, :])
            return 0

        lax.fori_loop(0, bounds[block, 1], k_block, 0)
        for h in range(heads):
            dqt_ref[h * HD : (h + 1) * HD, spot] = dq_ref[h].T * SCALE
        return 0

    lax.fori_loop(0, count // BQ, q_block, 0)
    width = heads * HD
    for item, (source, scale) in enumerate(((dqt_ref, 1.0), (dkt_ref, SCALE), (dvt_ref, 1.0))):
        value = source[...] if scale == 1.0 else source[...] * scale
        value = value.astype(BF16)
        flat_ref[item * width : (item + 1) * width, :] = value
    for part in range(parts):
        out_refs[part][...] = flat_ref[:, spot_of(layer, part, size)]


def attend_back(first, heads, layer, tables, q_rows, k_rows, q_cols, k_cols, v_cols, out, lse, dout):
    segr, bounds = tables
    count = segr.shape[1]
    parts = len(dout)
    width = heads * HD
    result = pl.pallas_call(
        partial(attend_back_kernel, first, heads, parts),
        in_specs=[pl.BlockSpec(memory_space=pltpu.SMEM)] * 2 + [vmem()] * (8 + parts),
        out_specs=[vmem()] * (parts + 1),
        out_shape=[jax.ShapeDtypeStruct((3 * width, count // parts), BF16)] * parts
        + [jax.ShapeDtypeStruct((3 * width, count), BF16)],
        scratch_shapes=[
            pltpu.VMEM((count, 128), F32),
            pltpu.VMEM((width, count), BF16),
            pltpu.VMEM((heads, count, HD), BF16),
            pltpu.VMEM((2 * heads, BQ, 128), F32),
            pltpu.VMEM((heads, BQ, HD), F32),
            pltpu.VMEM((width, count), F32),
            pltpu.VMEM((width, count), F32),
            pltpu.VMEM((width, count), F32),
        ],
        compiler_params=pltpu.CompilerParams(vmem_limit_bytes=VMEM_LIMIT),
        cost_estimate=COST,
        name=f"attend_back_{first}",
    )(layer, bounds, segr, q_rows, k_rows, q_cols, k_cols, v_cols, out, lse, *dout)
    return result[:parts], result[parts]


def mix_kernel(parts, layer, *refs):
    ot_refs, w_ref, refs = refs[:parts], refs[parts], refs[parts + 1 :]
    x_ref, gain_ref, shift_ref, x2_ref, xn_ref, ot_ref = refs
    middle = x_ref[...].astype(F32)
    for part in range(parts):
        value = ot_refs[part][...]
        ot_ref[layer[0] ^ part] = value
        middle = middle + dot(value.T, w_ref[layer[0] ^ part])
    x2_ref[...] = middle
    unit, _ = normalized(middle)
    xn_ref[...] = (unit * gain_ref[1:2, :].astype(F32) + shift_ref[1:2, :].astype(F32)).astype(BF16)


def mix(layer, ot, w_out, rows, gains, shifts):
    count, dim = rows.shape
    parts = len(ot)
    return pl.pallas_call(
        partial(mix_kernel, parts),
        in_specs=[pl.BlockSpec(memory_space=pltpu.SMEM)] + [vmem()] * (parts + 4),
        out_specs=[vmem()] * 3,
        out_shape=[
            jax.ShapeDtypeStruct((count, dim), F32),
            jax.ShapeDtypeStruct((count, dim), BF16),
            jax.ShapeDtypeStruct((parts,) + ot[0].shape, BF16),
        ],
        compiler_params=pltpu.CompilerParams(vmem_limit_bytes=VMEM_LIMIT),
        cost_estimate=COST,
        name="mix",
    )(layer, *ot, w_out, rows, gains, shifts)


def ffn_kernel(*refs):
    xn_parts, dy_parts, w_ref = refs[:2], refs[2:4], refs[4]
    outs, (g_ref, du_ref) = refs[5:9], refs[9:11]
    y_ref, dx_ref, xn_ref, dy_ref = refs[11:]
    item, side = pl.program_id(0), pl.program_id(1)
    mine, hidden = g_ref.shape
    spot = pl.ds(pl.multiple_of(side * mine, mine), mine)

    @pl.when((item == 0) & (side == 0))
    def _():
        for part in range(2):
            xn_ref[part * mine : (part + 1) * mine, :] = xn_parts[part][...]
            dy_ref[part * mine : (part + 1) * mine, :] = dy_parts[part][...]
        y_ref[...] = jnp.zeros_like(y_ref)
        dx_ref[...] = jnp.zeros_like(dx_ref)

    w_in, w_down = (w_ref[:, part].reshape(xn_ref.shape[1], hidden) for part in range(2))
    u = dot(xn_ref[spot, :], w_in)
    dg = dot(dy_ref[spot, :], w_down)
    half = 0.5 + 0.5 * lax.erf(u * 0.7071067811865476)
    slope = half + u * (jnp.exp2(u * u * (-0.5 * LOG2E)) * 0.3989422804014327)
    g = (u * half).astype(BF16)
    du = (dg * slope).astype(BF16)
    g_ref[...] = g
    du_ref[...] = du
    y_ref[spot, :] += dot_nt(g, w_down)
    dx_ref[spot, :] += dot_nt(du, w_in)

    @pl.when((item == pl.num_programs(0) - 1) & (side == 1))
    def _():
        outs[0][...] = y_ref[:mine, :].astype(BF16)
        outs[1][...] = dx_ref[:mine, :].astype(BF16)
        outs[2][...] = y_ref[mine:, :].astype(BF16)
        outs[3][...] = dx_ref[mine:, :].astype(BF16)


def ffn(xn, dy, weights):
    mine, dim = xn[0].shape
    count = 2 * mine
    _, _, tall, hidden = weights.shape
    depth = dim // tall
    blocks = weights.shape[0] // depth
    whole = pl.BlockSpec((mine, dim), lambda i, j: (0, 0))
    act = pl.BlockSpec((mine, hidden), lambda i, j: (j, i))
    return pl.pallas_call(
        ffn_kernel,
        grid=(blocks, 2),
        in_specs=[whole] * 4 + [pl.BlockSpec((depth, 2, tall, hidden), lambda i, j: (i, 0, 0, 0))],
        out_specs=[whole] * 4 + [act] * 2,
        out_shape=[jax.ShapeDtypeStruct((mine, dim), BF16)] * 4
        + [jax.ShapeDtypeStruct((count, blocks * hidden), BF16)] * 2,
        scratch_shapes=[pltpu.VMEM((count, dim), F32)] * 2 + [pltpu.VMEM((count, dim), BF16)] * 2,
        compiler_params=pltpu.CompilerParams(vmem_limit_bytes=VMEM_LIMIT),
        cost_estimate=COST,
        name="ffn",
    )(*xn, *dy, weights)


def outer_kernel(sides, _, *refs):
    xn_parts, dy_parts = refs[: 2 * sides], refs[2 * sides : 4 * sides]
    g_refs, du_refs = refs[4 * sides : 5 * sides], refs[5 * sides : 6 * sides]
    grad_ref, xnt_ref, dyt_ref = refs[6 * sides :]
    mine = xn_parts[0].shape[0]
    hidden = g_refs[0].shape[1]

    @pl.when(pl.program_id(0) == 0)
    def _():
        for part in range(2 * sides):
            xnt_ref[:, part * mine : (part + 1) * mine] = xn_parts[part][...].T
            dyt_ref[:, part * mine : (part + 1) * mine] = dy_parts[part][...].T

    for at, turned, sources in ((0, xnt_ref, du_refs), (hidden, dyt_ref, g_refs)):
        total = None
        for side in range(sides):
            cut = slice(2 * side * mine, 2 * (side + 1) * mine)
            term = dot(turned[:, cut], sources[side][...])
            total = term if total is None else total + term
        grad_ref[0, :, at : at + hidden] = total.astype(BF16)


def outer(base, xn, dy, g, du, hidden):
    sides = len(g)
    mine, dim = xn[0].shape
    count = 2 * mine
    blocks = g[0].shape[1] // hidden
    whole = pl.BlockSpec((mine, dim), lambda i, base: (0, 0))
    act = pl.BlockSpec((count, hidden), lambda i, base: (0, i ^ base[0]))
    return pl.pallas_call(
        partial(outer_kernel, sides),
        grid_spec=pltpu.PrefetchScalarGridSpec(
            num_scalar_prefetch=1,
            grid=(blocks,),
            in_specs=[whole] * (4 * sides) + [act] * (2 * sides),
            out_specs=pl.BlockSpec((1, dim, 2 * hidden), lambda i, base: (i, 0, 0)),
            scratch_shapes=[pltpu.VMEM((dim, sides * count), BF16)] * 2,
        ),
        out_shape=jax.ShapeDtypeStruct((blocks, dim, 2 * hidden), BF16),
        compiler_params=pltpu.CompilerParams(vmem_limit_bytes=VMEM_LIMIT),
        cost_estimate=COST,
        name="outer",
    )(base, *xn, *dy, *g, *du)


def turn_kernel(layer, w_ref, *refs):
    x2_ref, dx_ref, core_ref, near_ref, dy_ref, ot_ref, gain_ref = refs[:7]
    dx2_ref, gout_ref, sums_ref = refs[7:10]
    dot_refs = refs[10:]
    middle = x2_ref[...]
    grad = dx_ref[...].astype(F32) + core_ref[...].astype(F32) + near_ref[...].astype(F32)
    back, prod = norm_backward(middle, gain_ref[1:2, :].astype(F32), grad)
    dx2 = dy_ref[...].astype(F32) + back
    dx2_ref[...] = dx2
    sums_ref[...] = jnp.concatenate(
        [
            jnp.sum(prod, axis=0, keepdims=True),
            jnp.sum(grad, axis=0, keepdims=True),
            jnp.zeros((6, grad.shape[1]), F32),
        ],
        axis=0,
    )
    low = dx2.astype(BF16)
    across = low.T
    width = ot_ref.shape[1]
    for part in range(w_ref.shape[0]):
        dot_refs[part][...] = dot(w_ref[layer[0] ^ part], across).astype(BF16)
        gout_ref[:, part * width : (part + 1) * width] = dot_nt(across, ot_ref[part]).astype(BF16)


def turn(layer, w_out, x2, dx, core, near, dy, ot, gains):
    count, dim = x2.shape
    parts = w_out.shape[0]
    out = pl.pallas_call(
        turn_kernel,
        in_specs=[pl.BlockSpec(memory_space=pltpu.SMEM)] + [vmem()] * 8,
        out_specs=[vmem()] * (parts + 3),
        out_shape=[
            jax.ShapeDtypeStruct((count, dim), F32),
            jax.ShapeDtypeStruct((dim, dim), BF16),
            jax.ShapeDtypeStruct((8, dim), F32),
        ]
        + [jax.ShapeDtypeStruct(ot.shape[1:], BF16)] * parts,
        compiler_params=pltpu.CompilerParams(vmem_limit_bytes=VMEM_LIMIT),
        cost_estimate=COST,
        name="turn",
    )(layer, w_out, x2, dx, core, near, dy, ot, gains)
    return *out[:3], out[3:]


def finish_kernel(parts, layer, *refs):
    part_refs, refs = refs[:parts], refs[parts:]
    w_ref, x_ref, dx2_ref, gain_ref, out_ref = refs
    width = w_ref.shape[2]
    grad = None
    for part in range(parts):
        for item in range(3):
            value = part_refs[part][item * width : (item + 1) * width, :]
            term = dot(value.T, w_ref[layer[0] ^ part, item])
            grad = term if grad is None else grad + term
    back, _ = norm_backward(x_ref[...].astype(F32), gain_ref[0:1, :].astype(F32), grad)
    out_ref[...] = (dx2_ref[...] + back).astype(BF16)


def finish(layer, parts, w_qkv, rows, dx2, gains):
    count, dim = rows.shape
    return pl.pallas_call(
        partial(finish_kernel, len(parts)),
        in_specs=[pl.BlockSpec(memory_space=pltpu.SMEM)] + [vmem()] * (len(parts) + 4),
        out_specs=vmem(),
        out_shape=jax.ShapeDtypeStruct((count, dim), BF16),
        compiler_params=pltpu.CompilerParams(vmem_limit_bytes=VMEM_LIMIT),
        cost_estimate=COST,
        name="finish",
    )(layer, *parts, w_qkv, rows, dx2, gains)


def small_kernel(flat_ref, x_ref, w_ref, gain_ref, shift_ref, gout_ref, sums_ref, out_ref):
    dim = x_ref.shape[1]
    unit, _ = normalized(x_ref[...].astype(F32))
    inner = dot(flat_ref[...], unit.astype(BF16))
    sums = jnp.sum(flat_ref[...].astype(F32), axis=1, keepdims=True)
    grad = inner * gain_ref[0:1, :].astype(F32) + sums * shift_ref[0:1, :].astype(F32)
    width = w_ref.shape[1]
    gain = jnp.zeros((1, dim), F32)
    shift = jnp.zeros((1, dim), F32)
    for item in range(3):
        rows = slice(item * width, (item + 1) * width)
        w = w_ref[item].astype(F32)
        gain = gain + jnp.sum(w * inner[rows, :], axis=0, keepdims=True)
        shift = shift + jnp.sum(w * sums[rows, :], axis=0, keepdims=True)
    side = 3 * width
    out_ref[:, :dim] = gout_ref[...]
    out_ref[:, dim : dim + side] = grad.T.astype(BF16)
    sums = jnp.concatenate([gain, sums_ref[0:1, :], shift, sums_ref[1:2, :]], axis=0)
    sums = jnp.concatenate([sums, jnp.zeros((out_ref.shape[1] - dim - side - 4, dim), F32)], axis=0)
    out_ref[:, dim + side :] = sums.T.astype(BF16)


def small(flat, rows, w_qkv, gains, shifts, grad_out, sums):
    side, dim = flat.shape[0], rows.shape[1]
    total = -(-(dim + side + 8) // 128) * 128
    return pl.pallas_call(
        small_kernel,
        in_specs=[vmem()] * 7,
        out_specs=vmem(),
        out_shape=jax.ShapeDtypeStruct((dim, total), BF16),
        compiler_params=pltpu.CompilerParams(vmem_limit_bytes=VMEM_LIMIT),
        cost_estimate=COST,
        name="small",
    )(flat, rows, w_qkv, gains, shifts, grad_out, sums)


def collect_kernel(layer, *refs):
    parts, out_ref = refs[:-1], refs[-1]
    size = parts[0].shape[0]
    for item, part in enumerate(parts):
        out_ref[pl.ds(pl.multiple_of((layer[0] ^ item) * size, 128), size), :] = part[...]


def collect(layer, parts):
    size, dim = parts[0].shape
    return pl.pallas_call(
        collect_kernel,
        in_specs=[pl.BlockSpec(memory_space=pltpu.SMEM)] + [vmem()] * len(parts),
        out_specs=vmem(),
        out_shape=jax.ShapeDtypeStruct((size * len(parts), dim), parts[0].dtype),
        compiler_params=pltpu.CompilerParams(vmem_limit_bytes=VMEM_LIMIT),
        cost_estimate=COST,
        name="collect",
    )(layer, *parts)


def keep_kernel(source_ref, out_ref):
    out_ref[...] = source_ref[...]


def keep(value):
    return pl.pallas_call(
        keep_kernel,
        in_specs=[vmem()],
        out_specs=vmem(),
        out_shape=jax.ShapeDtypeStruct(value.shape, value.dtype),
        compiler_params=pltpu.CompilerParams(vmem_limit_bytes=VMEM_LIMIT),
        cost_estimate=COST,
        name="keep",
    )(value)


WIDE = ("far", "near", "core")


def swap(value, axis):
    return lax.ppermute(value, axis, [(0, 1), (1, 0)])


def spread(parts):
    size = len(parts)
    return [parts[0]] + [
        lax.ppermute(parts[bit], "narrow", [(i, i ^ bit) for i in range(size)])
        for bit in range(1, size)
    ]


def exchange(value, axis):
    return lax.all_to_all(value, axis, 0, 0, tiled=True)


def after(value, *others):
    return lax.optimization_barrier((value,) + others)[0]


def add(*parts):
    return sum(part.astype(F32) for part in parts).astype(BF16)


def local(
    tokens, cotangent, seq_lens, norm_gains, norm_shifts, w_qkv, w_attn_out, w_ffn_in, w_ffn_down
):
    depth = lax.axis_size("narrow")
    across = lax.axis_size(WIDE)
    count, dim = tokens.shape
    mine = count // depth
    width = w_qkv.shape[2]
    cols = w_ffn_in.shape[1]
    heads = width // HD
    layer = lax.axis_index("narrow")
    layers = layer.astype(jnp.int32).reshape(1)

    pieces = lax.all_gather(
        jnp.concatenate([w_qkv.transpose(2, 0, 1).reshape(width, -1), w_attn_out], axis=1),
        WIDE,
        axis=0,
    )
    weights = lax.all_gather(jnp.stack([w_ffn_in, w_ffn_down]), ("far", "narrow"), axis=0)
    group = max(1, dim // cols)
    if group > 1:
        weights = weights.reshape((-1, group, depth) + weights.shape[1:])
        weights = weights.transpose(0, 2, 3, 4, 1, 5).reshape(-1, 2, dim // depth, group * cols)
    rows = lax.dynamic_slice_in_dim(tokens, layer * mine, mine, 0)
    dy = lax.dynamic_slice_in_dim(cotangent, layer * mine, mine, 0)
    dy_near = swap(dy, "near")
    dy_own = (dy, swap(dy, "core"))
    dy_far = (dy_near, swap(dy_near, "core"))

    q_rows, k_rows, q_cols, k_cols, v_cols, *tables, w_proj, w_out = project(
        seq_lens, tokens, norm_gains, norm_shifts, pieces, depth
    )
    w_out = exchange(w_out, "narrow")
    parts, out, lse = attend(0, heads, depth, layers, tables, k_rows, q_cols, v_cols)
    x2, xn2, ot = mix(layers, spread(parts), w_out, rows, norm_gains, norm_shifts)
    xn_near = swap(xn2, "near")
    xn_own = (xn2, swap(xn2, "core"))
    w_proj_all = lax.all_gather(w_proj, "narrow", axis=0)

    y_a, dx_a, y_core, dx_core, g_a, du_a = ffn(xn_own, dy_own, weights)
    xn_near = after(xn_near, y_a)
    xn_far = (xn_near, swap(xn_near, "core"))
    y_b, dx_b, y_far, dx_far, g_b, du_b = ffn(xn_far, dy_far, weights)
    dx_core = swap(dx_core, "core")
    dx_near = swap(add(dx_b, swap(dx_far, "core")), "near")
    pair = lax.axis_size("far") == 2
    base = lax.axis_index("far") if pair else jnp.zeros((), jnp.int32)
    base = base.astype(jnp.int32).reshape(1)
    grads = outer(base, xn_own + xn_far, dy_own + dy_far, (g_a, g_b), (du_a, du_b), group * cols)
    dx2, grad_out, norm_two, dout = turn(
        layers, w_out, after(x2, grads), dx_a, dx_core, dx_near, dy, ot, norm_gains
    )
    dout = spread(dout)
    y_core, y_far = (swap(part, "core") for part in (y_core, y_far))
    y_near = swap(add(y_b, y_far), "near")
    out_mine = x2 + y_a.astype(F32) + y_core.astype(F32) + y_near.astype(F32)
    out_mine = out_mine.astype(BF16)
    dout, out_mine = lax.optimization_barrier((dout, out_mine))
    layer_out = lax.all_gather(out_mine, "narrow", axis=0, tiled=True)
    back, flat_back = attend_back(
        0, heads, layers, tables, q_rows, k_rows, q_cols, k_cols, v_cols, out, lse, dout
    )
    if pair:
        back, far_grads = lax.optimization_barrier((back, swap(grads[1], "far")))
        total = add(after(grads[0], flat_back), far_grads)
    else:
        grads = grads.reshape(-1, dim, 2, group, cols).transpose(0, 3, 1, 2, 4)
        grads = grads.reshape(-1, dim, 2 * cols)
        total = lax.psum_scatter(grads, "far", scatter_dimension=0, tiled=False)
    total = lax.psum_scatter(total, "narrow", scatter_dimension=0, tiled=True).astype(F32)

    back = spread(back)
    rest = small(flat_back, tokens, w_proj, norm_gains, norm_shifts, grad_out, norm_two)
    in_mine = finish(layers, back, w_proj_all, rows, after(dx2, rest), norm_gains)
    input_grad = lax.all_gather(in_mine, "narrow", axis=0, tiled=True)

    side = 3 * width
    part = dim // across
    rest = exchange(after(rest, in_mine).reshape(across, part, -1), WIDE)
    rest = jnp.sum(rest.astype(F32), axis=0)
    layer_out = keep(after(layer_out, rest))
    gqkv = rest[:, dim : dim + side].reshape(part, 3, width).transpose(1, 0, 2)
    gout = rest[:, :dim].astype(BF16).reshape(part, depth, width).transpose(1, 0, 2)
    norms = rest[:, dim + side : dim + side + 4].astype(BF16)
    gout = jnp.concatenate([gout, jnp.broadcast_to(norms, (depth, part, 4))], axis=2)
    gout = jnp.sum(exchange(gout, "narrow").astype(F32), axis=0).T
    gout, norms = gout[:width], gout[width:]
    return (
        layer_out,
        input_grad,
        norms[:2],
        norms[2:],
        gqkv,
        gout,
        total[:, :cols],
        total[:, cols:],
    )


def solution(mesh):
    depth, across = mesh.shape["narrow"], mesh.shape["wide"]
    fine = jax.sharding.Mesh(
        mesh.devices.reshape(depth, across // 4, 2, 2), ("narrow", "far", "near", "core")
    )
    return jax.shard_map(
        local,
        mesh=fine,
        in_specs=(
            P(WIDE, None),
            P(WIDE, None),
            P(WIDE, None),
            P(),
            P(),
            P(None, WIDE, "narrow"),
            P("narrow", WIDE),
            P("narrow", WIDE),
            P("narrow", WIDE),
        ),
        out_specs=(
            P(WIDE, None),
            P(WIDE, None),
            P(None, WIDE),
            P(None, WIDE),
            P(None, WIDE, "narrow"),
            P("narrow", WIDE),
            P("narrow", WIDE),
            P("narrow", WIDE),
        ),
        check_vma=False,
    )
```
